32 devices in a mesh: seq: 2 (over y), dom: 8 (over z, x), tm: 2 (over core).
Axes of the slice: x: 2, y: 2, z: 4, core: 2. Of those that a mesh axis runs over, the one named last changes fastest.
Arguments:
- particles: bfloat16 [4, 1536, 128], P('tm', ('seq', 'dom')), parts along dimension 1, may hold values from -6 to 6
- log_weight: float32 [4, 1536], P('tm', ('seq', 'dom')), parts along dimension 1, may hold values from -13 to 313
- trans_weight: bfloat16 [128, 128], replicated, may hold values from -0.5 to 0.5
- precision: float32 [128], replicated, may hold values from 0.2 to 2
Outputs:
- smoothed: float32 [4, 1536], P('tm', ('seq', 'dom')), parts along dimension 1
- score: float32 [256, 128], P('seq'), parts along dimension 0
The draws below stay inside these ranges and needn't reach their ends.
There are 2 independent parts, one for each index of `seq`. The reference program is written for one: setup_inputs(seed, part) draws one part's arguments, and reference() takes and returns one part's arrays. A program takes and returns all parts, laid end to end along the dimension named above; an argument that names none is the same for every part. Nothing has to cross between parts.
All inputs are finite; a program needn't handle non-finite values.
Results may differ from the reference program's by a relative error of at most 0.0061.
Values may be sent and summed in bfloat16 or wider, within the bound.
A program may use at most 64 MiB of HBM per device.

```python
import math
import jax
import jax.numpy as jnp
from jax import lax

D = 128
N_DEV = 96
N = 768
WINDOW = 4
N_DOM = 8


def draw_log_weight(key, part):
    base_key, shift_key = jax.random.split(key)
    base = jax.random.truncated_normal(base_key, -5.0, 5.0, (WINDOW, N), jnp.float32) * 1.5
    offset = jax.random.uniform(shift_key, (WINDOW,), jnp.float32, -4.0, 4.0)
    return base + offset[:, None]


def block_scale(key, extent, cuts, least, top_value):
    def one(position, blocks):
        heights = jax.random.uniform(jax.random.fold_in(jax.random.fold_in(key, 6), position), (blocks,), jnp.float32, least / len(cuts), top_value / len(cuts))
        return jnp.repeat(jnp.exp(heights), extent[position] // blocks).reshape((-1,) + (1,) * (len(extent) - position - 1))

    level = one(*cuts[0])
    for cut in cuts[1:]:
        level = level * one(*cut)
    return level


def gaussian(key, shape, scale, most, shards=(), kind=jnp.bfloat16):
    values = jax.random.normal(key, shape, jnp.float32) * scale
    if len(shards) > 0:
        values = block_scale(key, shape, shards, -0.22, 0.18) * values
    return jnp.clip(values, min=-most, max=most).astype(kind)


def setup_inputs(seed: int = 0, part: int = 0) -> dict:
    keys = jax.random.split(jax.random.key(seed), 5)
    own_keys = jax.random.split(jax.random.fold_in(keys[4], part), 5)
    particles = gaussian(own_keys[0], (WINDOW, N, D), 1.0, 6.0, ((0, 2), (1, 8)))
    log_weight = draw_log_weight(jax.random.fold_in(jax.random.fold_in(keys[4], part), 71), part)
    trans_weight = gaussian(keys[2], (D, D), D ** -0.5, 0.5)
    precision = jnp.clip(jnp.exp(jax.random.uniform(keys[3], (D,), jnp.float32, math.log(0.2), math.log(2.0))), 0.2, 2.0)
    return dict(particles=particles, log_weight=log_weight, trans_weight=trans_weight, precision=precision)


def reference(particles, log_weight, trans_weight, precision):
    exact_mode = lax.Precision.HIGHEST
    weight_full = trans_weight.astype(jnp.float32)
    width = particles.shape[2]
    total_rows = particles.shape[1]
    final_logs = log_weight[WINDOW - 1]
    highest = jnp.max(final_logs)
    expanded = jnp.exp(final_logs - highest)
    smoothed = [None] * WINDOW
    smoothed[WINDOW - 1] = expanded / jnp.sum(expanded)
    score = jnp.zeros((width, width), jnp.float32)
    for t in range(WINDOW - 2, -1, -1):
        columns = particles[t]
        later = particles[t + 1]
        predicted = jnp.dot(columns, trans_weight.T, preferred_element_type=jnp.float32)
        column_bias = log_weight[t] - 0.5 * jnp.sum(precision * predicted * predicted, axis=1)
        projected = jnp.dot(later.astype(jnp.float32) * precision, weight_full, precision=exact_mode).astype(jnp.bfloat16)
        blocks = (projected.reshape(N_DOM, N_DEV, width), smoothed[t + 1].reshape(N_DOM, N_DEV), later.reshape(N_DOM, N_DEV, width))

        def accumulate(carried, block):
            column_sums, outer = carried
            proj_block, weight_block, later_block = block
            scores = jnp.dot(proj_block, columns.T, preferred_element_type=jnp.float32) + column_bias[None, :]
            row_top = jnp.max(scores, axis=1)
            row_norm = row_top + jnp.log(jnp.sum(jnp.exp(scores - row_top[:, None]), axis=1))
            backward = (weight_block[:, None] * jnp.exp(scores - row_norm[:, None])).astype(jnp.bfloat16)
            column_sums = column_sums + jnp.sum(backward.astype(jnp.float32), axis=0)
            moved = jnp.dot(backward, columns, preferred_element_type=jnp.float32)
            outer = outer + jnp.dot(later_block.astype(jnp.float32).T, moved, precision=exact_mode)
            return (column_sums, outer), None

        start_state = (jnp.zeros((total_rows,), jnp.float32), jnp.zeros((width, width), jnp.float32))
        (column_sums, outer), unused = lax.scan(accumulate, start_state, blocks)
        column_float = columns.astype(jnp.float32)
        moment = jnp.dot(column_float.T * column_sums[None, :], column_float, precision=exact_mode)
        score = score + precision[:, None] * (outer - jnp.dot(weight_full, moment, precision=exact_mode))
        smoothed[t] = column_sums
    return jnp.stack(smoothed) * total_rows, score
```

```python
import functools

import jax
import jax.numpy as jnp
from jax import lax
from jax.experimental import pallas as pl
from jax.experimental.pallas import tpu as pltpu
from jax.sharding import PartitionSpec as P

exact_mode = lax.Precision.HIGHEST


def from_behind(x, axis, by):
    size = lax.axis_size(axis)
    pairs = [(i, i + by) for i in range(size) if 0 <= i + by < size]
    return lax.ppermute(x, axis, pairs)


def block_size(length):
    best = 1
    for trial in range(1, min(length, 512) + 1):
        if length % trial == 0:
            best = trial
    return best


def project_rows(rows, precision, weight_full):
    return jnp.dot(rows.astype(jnp.float32) * precision, weight_full, precision=exact_mode).astype(
        jnp.bfloat16
    )


def pair_scores(row_proj, column_rows, column_bias):
    return (
        jnp.einsum("id,jd->ij", row_proj, column_rows, preferred_element_type=jnp.float32)
        + column_bias[None, :]
    )


def make_norm_fold(row_proj, bias_row, carried, block_in, first_row):
    length = block_in.shape[0]
    size = block_size(length)

    def inner(position, state):
        row_top, row_total = state
        offset = position * size
        column_rows = lax.dynamic_slice_in_dim(block_in, offset, size, 0)
        bias_part = lax.dynamic_slice_in_dim(bias_row, first_row + offset, size, 0)
        scores = pair_scores(row_proj, column_rows, bias_part)
        new_top = jnp.maximum(row_top, jnp.max(scores, axis=1))
        row_total = row_total * jnp.exp(row_top - new_top) + jnp.sum(
            jnp.exp(scores - new_top[:, None]), axis=1
        )
        return (new_top, row_total)

    return lax.fori_loop(0, length // size, inner, carried)


def make_column_fold(row_proj, bias_row, row_norm, row_weight, carried, block_in, first_row):
    length = block_in.shape[0]
    size = block_size(length)

    def inner(position, state):
        moved, column_sums = state
        offset = position * size
        column_rows = lax.dynamic_slice_in_dim(block_in, offset, size, 0)
        bias_part = lax.dynamic_slice_in_dim(bias_row, first_row + offset, size, 0)
        scores = pair_scores(row_proj, column_rows, bias_part)
        backward = (row_weight[:, None] * jnp.exp(scores - row_norm[:, None])).astype(jnp.bfloat16)
        moved = moved + jnp.dot(backward, column_rows, preferred_element_type=jnp.float32)
        column_sums = lax.dynamic_update_slice_in_dim(
            column_sums, jnp.sum(backward.astype(jnp.float32), axis=0), first_row + offset, 0
        )
        return (moved, column_sums)

    return lax.fori_loop(0, length // size, inner, carried)


def shards(particles, log_weight, trans_weight, precision):
    steps_here, rows_here, width = particles.shape
    tm_count = lax.axis_size("tm")
    dom_count = lax.axis_size("dom")
    total_rows = rows_here * dom_count
    tm_place = lax.axis_index("tm")
    is_last = tm_place == tm_count - 1
    weight_full = trans_weight.astype(jnp.float32)
    boundary = from_behind(particles[0], "tm", -1)
    later_sets = [particles[1]] + [boundary]
    later_proj = [project_rows(rows, precision, weight_full) for rows in later_sets]
    biases = []
    for k in range(steps_here):
        predicted = jnp.dot(particles[k], trans_weight.T, preferred_element_type=jnp.float32)
        biases.append(log_weight[k] - 0.5 * jnp.sum(precision * predicted * predicted, axis=1))
    local_bias = jnp.stack(biases)
    full_bias = lax.all_gather(local_bias, "dom", axis=1, tiled=True)
    row_norms = []
    whole = lax.all_gather(particles, "dom", axis=1, tiled=True)
    for k in range(steps_here):
        start_state = (
            jnp.full((rows_here,), -jnp.inf, jnp.float32),
            jnp.zeros((rows_here,), jnp.float32),
        )
        row_top, row_total = make_norm_fold(later_proj[k], full_bias[k], start_state, whole[k], 0)
        row_norms.append(row_top + jnp.log(row_total))
    final_logs = log_weight[steps_here - 1]
    global_top = lax.pmax(jnp.max(final_logs), "dom")
    global_total = lax.psum(jnp.sum(jnp.exp(final_logs - global_top)), "dom")
    final_weights = jnp.exp(final_logs - global_top) / global_total
    carried = (
        jnp.zeros((steps_here, rows_here), jnp.float32),
        jnp.zeros((width, width), jnp.float32),
    )
    for r in range(tm_count):
        if r == 0:
            incoming = jnp.zeros((rows_here,), jnp.float32)
        else:
            incoming = from_behind(carried[0][0], "tm", -1)
        owner = tm_count - 1 - r
        backward_partial_value = jnp.zeros((width, width), jnp.float32)
        outputs = [None] * steps_here
        row_weight = incoming
        for backward_k in range(steps_here - 1, -1, -1):
            column_rows = particles[backward_k]
            backward_start_state = (
                jnp.zeros((rows_here, width), jnp.float32),
                jnp.zeros((total_rows,), jnp.float32),
            )
            moved, column_sums = make_column_fold(
                later_proj[backward_k],
                full_bias[backward_k],
                row_norms[backward_k],
                row_weight,
                backward_start_state,
                whole[backward_k],
                0,
            )
            column_weights = lax.psum_scatter(column_sums, "dom", scatter_dimension=0, tiled=True)
            outer = jnp.dot(
                later_sets[backward_k].astype(jnp.float32).T, moved, precision=exact_mode
            )
            column_float = column_rows.astype(jnp.float32)
            moment = jnp.dot(
                column_float.T * column_weights[None, :], column_float, precision=exact_mode
            )
            backward_partial_value = backward_partial_value + precision[:, None] * (
                outer - jnp.dot(weight_full, moment, precision=exact_mode)
            )
            if backward_k == steps_here - 1:
                column_weights = jnp.where(is_last, final_weights, column_weights)
            outputs[backward_k] = column_weights
            row_weight = column_weights
        is_owner = tm_place == owner
        carried = (
            jnp.where(is_owner, jnp.stack(outputs), carried[0]),
            jnp.where(is_owner, backward_partial_value, carried[1]),
        )
    stacked, partial_value = carried
    score = lax.psum(partial_value, ("dom", "tm"))
    return (stacked * total_rows, score)


MESH = pl.DeviceIdType.MESH
EXTRA = 16
MOST_ROWS = 1024


def nt_dot(a, b):
    return lax.dot_general(a, b, (((1,), (1,)), ((), ())), preferred_element_type=jnp.float32)


def tn_dot(a, b):
    return lax.dot_general(a, b, (((0,), (0,)), ((), ())), preferred_element_type=jnp.float32)


def nn_dot(a, b):
    return jnp.dot(a, b, preferred_element_type=jnp.float32)


def split_three(x):
    high = x.astype(jnp.bfloat16)
    rest = x - high.astype(jnp.float32)
    middle = rest.astype(jnp.bfloat16)
    low = (rest - middle.astype(jnp.float32)).astype(jnp.bfloat16)
    return high, middle, low


def smoother_kernel(
    n_dom, x_hbm, lw_hbm, w_hbm, p_hbm, smoothed_ref, score_ref,
    lw_ref, w_ref, p_ref, held, kernel_rows, stats, inverse_norm, bias, weights, stage, in_sem, send_sem, recv_sem,
):
    rows, width = x_hbm.shape[1:]
    total = n_dom * rows
    steps = 4
    half = total // 2
    dom = lax.axis_index("dom")
    tm = lax.axis_index("tm")
    group, side = dom // 2, dom % 2
    high, low = group // 2, group % 2
    near = 2 * high + 1 - low
    mirror = 2 * (1 - high) + low
    opposite = 2 * (1 - high) + 1 - low
    across = dom + 1 - 2 * side
    other = 1 - tm
    mine = tm * n_dom + group
    peers = [2 * g + side for g in (near, mirror, opposite)]

    loads = [
        pltpu.make_async_copy(source, target, in_sem.at[i])
        for i, (source, target) in enumerate(
            [
                (w_hbm, w_ref),
                (p_hbm, p_ref),
                (lw_hbm, lw_ref),
                (x_hbm.at[0], held.at[mine, 0:rows]),
                (x_hbm.at[1], held.at[mine, rows : 2 * rows]),
            ]
        )
    ]
    for load in loads:
        load.start()

    barrier = pltpu.get_barrier_semaphore()
    targets = [(peer, tm) for peer in peers] + [(across, tm), (dom, other)]
    for to_dom, to_tm in targets:
        pl.semaphore_signal(
            barrier, inc=1, device_id={"dom": to_dom, "tm": to_tm}, device_id_type=MESH
        )

    for load in loads:
        load.wait()
    weight = w_ref[...]
    p_row = p_ref[...]
    p_down = jnp.broadcast_to(p_row, (width, width)).T
    stage[...] = jnp.zeros_like(stage)
    terms = []
    for k in range(2):
        x_k = held[mine, k * rows : (k + 1) * rows, :]
        predicted = nt_dot(weight, x_k)
        energy = jnp.sum(p_down[:, :rows] * predicted * predicted, axis=0, keepdims=True)
        terms.append(lw_ref[k : k + 1, :] - 0.5 * energy)
    terms.append(lw_ref[1:2, :])
    for q in range(3):
        for piece, value in enumerate(split_three(terms[q])):
            row = 3 * piece + q
            stage[row : row + 1, 0:rows] = value.astype(jnp.float32)
    held[mine, 2 * rows : 2 * rows + EXTRA, :] = stage[...].astype(jnp.bfloat16)

    pl.semaphore_wait(barrier, len(targets))

    sends = []

    def transfer(source, target, index, to_dom, to_tm):
        return pltpu.make_async_remote_copy(
            src_ref=held.at[source],
            dst_ref=held.at[target],
            send_sem=send_sem.at[index],
            recv_sem=recv_sem.at[target],
            device_id={"dom": to_dom, "tm": to_tm},
            device_id_type=MESH,
        )

    def send(source, target, to_dom, to_tm):
        copy = transfer(source, target, len(sends), to_dom, to_tm)
        copy.start()
        sends.append(copy)

    def arrive(slot):
        transfer(slot, slot, 0, dom, other).wait_recv()

    base, far_base = tm * n_dom, other * n_dom
    part = n_dom // 2
    for peer in peers:
        send(mine, mine, peer, tm)
    send(mine, mine + part, across, tm)
    send(mine, mine, dom, other)

    scaled = jnp.concatenate(split_three(p_down * weight.astype(jnp.float32)), axis=1)
    line = lax.broadcasted_iota(jnp.int32, (EXTRA, 3 * width), 0)
    which = lax.broadcasted_iota(jnp.int32, (EXTRA, 3 * width), 1) // width
    pick = jnp.where((line < 9) & (line % 3 == which), 1.0, 0.0).astype(jnp.bfloat16)

    def set_of(at, k):
        return held[pl.ds(at, part), k * rows : (k + 1) * rows, :].reshape(half, width)

    def spread_bias(h):
        for c in range(2):
            for g in range(part):
                s = c * n_dom + h * part + g
                spread = tn_dot(held[s, 2 * rows : 2 * rows + EXTRA, :], pick)
                for k in range(2):
                    t = 2 * c + k
                    q = 2 if t == steps - 1 else k
                    bias[t, h, g * rows : (g + 1) * rows, :] = spread[:rows, q * width : (q + 1) * width]

    def tile(t, column_at, column_k, row_at, row_k, j, i):
        wide = nn_dot(set_of(row_at + i * part, row_k), scaled)
        projected = (
            wide[:, :width] + (wide[:, width : 2 * width] + wide[:, 2 * width :])
        ).astype(jnp.bfloat16)
        scores = nt_dot(set_of(column_at + j * part, column_k), projected)
        scores = scores + jnp.concatenate([bias[t, j]] * (half // width), axis=1)
        top = jnp.max(scores, axis=0, keepdims=True)
        terms = jnp.exp(scores - top)
        kernel_rows[t, j, :, i * half : (i + 1) * half] = terms.astype(jnp.bfloat16)
        stats[t, 2 * j + i, 0:1, :] = top
        stats[t, 2 * j + i, 1:2, :] = jnp.sum(terms, axis=0, keepdims=True)

    def tall_tile(t, column_at, column_k, row_at, row_k):
        wide = nn_dot(set_of(row_at + part, row_k), scaled)
        projected = (
            wide[:, :width] + (wide[:, width : 2 * width] + wide[:, 2 * width :])
        ).astype(jnp.bfloat16)
        columns = [set_of(column_at + j * part, column_k) for j in range(2)]
        scores = nt_dot(jnp.concatenate(columns, axis=0), projected)
        column_bias = bias[t].reshape(total, width)
        scores = scores + jnp.concatenate([column_bias] * (half // width), axis=1)
        top = jnp.max(scores, axis=0, keepdims=True)
        terms = jnp.exp(scores - top)
        rounded = terms.astype(jnp.bfloat16)
        sums = (jnp.sum(terms, axis=0, keepdims=True), jnp.zeros_like(top))
        for j in range(2):
            kernel_rows[t, j, :, half:] = rounded[j * half : (j + 1) * half]
            stats[t, 2 * j + 1, 0:1, :] = top
            stats[t, 2 * j + 1, 1:2, :] = sums[j]

    own_t = (2 * tm, base, 0, base, 1)
    middle_t = (1, 0, 1, n_dom, 0)
    other_t = (2 * other, far_base, 0, far_base, 1)

    for n, g in enumerate((near, mirror, opposite)):
        arrive(base + g)
        send(base + g, base + g + part, across, tm)
        send(base + g, base + g, dom, other)
        if n == 0:
            arrive(base + part + group)
            send(base + part + group, base + part + group, dom, other)
    for g in range(part):
        arrive(far_base + g)
    spread_bias(0)
    for case in (own_t, middle_t, other_t):
        tile(*case, 0, 0)
    for g in (near, mirror, opposite):
        arrive(base + part + g)
        send(base + part + g, base + part + g, dom, other)
    for g in range(part):
        arrive(far_base + part + g)
    spread_bias(1)

    last = bias[steps - 1].reshape(total, width)
    last = jnp.exp(last - jnp.max(last, axis=0, keepdims=True))
    weights[steps - 1] = last / jnp.sum(last, axis=0, keepdims=True)

    for case in (own_t, middle_t, other_t):
        tile(*case, 1, 0)
        tall_tile(*case)

    score = jnp.zeros((width, width), jnp.float32)
    for t in range(steps - 2, -1, -1):
        for i in range(2):
            tops = [stats[t, 2 * j + i, 0:1, :] for j in range(2)]
            top = jnp.maximum(tops[0], tops[1])
            scales = [jnp.exp(tops[j] - top) for j in range(2)]
            norm = sum(scales[j] * stats[t, 2 * j + i, 1:2, :] for j in range(2))
            for j in range(2):
                inverse = scales[j] / norm
                for b in range(half // width):
                    at = i * half + b * width
                    inverse_norm[t, j, at : at + width, :] = jnp.broadcast_to(
                        inverse[:, b * width : (b + 1) * width], (width, width)
                    ).T
    for t in range(steps - 2, -1, -1):
        at, k = (t // 2) * n_dom, t % 2
        later_at, later_k = ((t + 1) // 2) * n_dom, (t + 1) % 2
        later = jnp.concatenate([set_of(later_at + i * part, later_k) for i in range(2)], axis=0)
        later = later.astype(jnp.float32)
        for j in range(2):
            ratio = weights[t + 1] * inverse_norm[t, j]
            right = jnp.concatenate(
                [(ratio * later).astype(jnp.bfloat16), ratio.astype(jnp.bfloat16)], axis=1
            )
            both = nn_dot(kernel_rows[t, j], right)
            now = both[:, width:]
            weights[t, j * half : (j + 1) * half, :] = now
            columns = set_of(at + j * part, k)
            predicted = nt_dot(columns, weight)
            residual = (both[:, :width] - predicted * now).astype(jnp.bfloat16)
            score = score + tn_dot(residual, columns)
    score_ref[...] = score * p_down
    first = pl.multiple_of(group * rows, rows)
    for k in range(2):
        own = weights[2 * tm + k, pl.ds(first, rows), :]
        smoothed_ref[k : k + 1, :] = own.T[0:1, :] * total
    for copy in sends:
        copy.wait_send()


def hand_over(a_in, b_in, a_out, b_out, sems):
    leaving = [
        pltpu.make_async_copy(a_in, a_out, sems.at[0]),
        pltpu.make_async_copy(b_in, b_out, sems.at[1]),
    ]
    for copy in leaving:
        copy.start()
    for copy in leaving:
        copy.wait()


def fused(particles, log_weight, trans_weight, precision):
    steps_here, rows, width = particles.shape
    n_dom = lax.axis_size("dom")
    total = n_dom * rows
    whole = pl.BlockSpec(memory_space=pltpu.VMEM)
    copies = (n_dom // 2 - 1) * 3 + 2 + n_dom // 2
    smoothed, score = pl.pallas_call(
        functools.partial(smoother_kernel, n_dom),
        out_shape=(
            pltpu.VMEM((steps_here, rows), jnp.float32),
            pltpu.VMEM((width, width), jnp.float32),
        ),
        in_specs=[pl.BlockSpec(memory_space=pltpu.HBM)] * 4,
        out_specs=(whole, whole),
        scratch_shapes=[
            pltpu.VMEM((steps_here, rows), jnp.float32),
            pltpu.VMEM((width, width), jnp.bfloat16),
            pltpu.VMEM((1, width), jnp.float32),
            pltpu.VMEM((2 * n_dom, 2 * rows + EXTRA, width), jnp.bfloat16),
            pltpu.VMEM((3, 2, total // 2, total), jnp.bfloat16),
            pltpu.VMEM((3, 4, 8, total // 2), jnp.float32),
            pltpu.VMEM((3, 2, total, width), jnp.float32),
            pltpu.VMEM((4, 2, total // 2, width), jnp.float32),
            pltpu.VMEM((4, total, width), jnp.float32),
            pltpu.VMEM((EXTRA, width), jnp.float32),
            pltpu.SemaphoreType.DMA((5,)),
            pltpu.SemaphoreType.DMA((copies,)),
            pltpu.SemaphoreType.DMA((2 * n_dom,)),
        ],
        compiler_params=pltpu.CompilerParams(
            collective_id=0, has_side_effects=True, vmem_limit_bytes=40 * 2**20
        ),
    )(*[pltpu.with_memory_space_constraint(a, pltpu.HBM) for a in (particles, log_weight, trans_weight, precision.reshape(1, width))])
    return pl.pallas_call(
        hand_over,
        out_shape=(
            jax.ShapeDtypeStruct((steps_here, rows), jnp.float32),
            jax.ShapeDtypeStruct((width, width), jnp.float32),
        ),
        in_specs=[whole] * 2,
        out_specs=(pl.BlockSpec(memory_space=pltpu.HBM),) * 2,
        scratch_shapes=[
            pltpu.SemaphoreType.DMA((2,)),
        ],
        compiler_params=pltpu.CompilerParams(vmem_limit_bytes=40 * 2**20),
    )(smoothed, score)


def plan(particles, log_weight, trans_weight, precision):
    steps_here, rows, width = particles.shape
    n_dom = lax.axis_size("dom")
    total = n_dom * rows
    small = total <= MOST_ROWS and total % (2 * width) == 0 and rows <= width and rows % 16 == 0
    shaped = n_dom == 8 and lax.axis_size("tm") == 2 and steps_here == 2 and width == 128
    if small and shaped:
        return fused(particles, log_weight, trans_weight, precision)
    return shards(particles, log_weight, trans_weight, precision)


def solution(mesh):
    placed = (P("tm", ("seq", "dom"), None), P("tm", ("seq", "dom")), P(), P())
    return jax.shard_map(
        plan,
        mesh=mesh,
        in_specs=placed,
        out_specs=(P("tm", ("seq", "dom")), P("seq", None)),
        check_vma=False,
    )
```

```python
import functools

import jax
import jax.numpy as jnp
from jax import lax
from jax.experimental import pallas as pl
from jax.experimental.pallas import tpu as pltpu
from jax.sharding import PartitionSpec as P

exact_mode = lax.Precision.HIGHEST


def from_behind(x, axis, by):
    size = lax.axis_size(axis)
    pairs = [(i, i + by) for i in range(size) if 0 <= i + by < size]
    return lax.ppermute(x, axis, pairs)


def block_size(length):
    best = 1
    for trial in range(1, min(length, 512) + 1):
        if length % trial == 0:
            best = trial
    return best


def project_rows(rows, precision, weight_full):
    return jnp.dot(rows.astype(jnp.float32) * precision, weight_full, precision=exact_mode).astype(
        jnp.bfloat16
    )


def pair_scores(row_proj, column_rows, column_bias):
    return (
        jnp.einsum("id,jd->ij", row_proj, column_rows, preferred_element_type=jnp.float32)
        + column_bias[None, :]
    )


def make_norm_fold(row_proj, bias_row, carried, block_in, first_row):
    length = block_in.shape[0]
    size = block_size(length)

    def inner(position, state):
        row_top, row_total = state
        offset = position * size
        column_rows = lax.dynamic_slice_in_dim(block_in, offset, size, 0)
        bias_part = lax.dynamic_slice_in_dim(bias_row, first_row + offset, size, 0)
        scores = pair_scores(row_proj, column_rows, bias_part)
        new_top = jnp.maximum(row_top, jnp.max(scores, axis=1))
        row_total = row_total * jnp.exp(row_top - new_top) + jnp.sum(
            jnp.exp(scores - new_top[:, None]), axis=1
        )
        return (new_top, row_total)

    return lax.fori_loop(0, length // size, inner, carried)


def make_column_fold(row_proj, bias_row, row_norm, row_weight, carried, block_in, first_row):
    length = block_in.shape[0]
    size = block_size(length)

    def inner(position, state):
        moved, column_sums = state
        offset = position * size
        column_rows = lax.dynamic_slice_in_dim(block_in, offset, size, 0)
        bias_part = lax.dynamic_slice_in_dim(bias_row, first_row + offset, size, 0)
        scores = pair_scores(row_proj, column_rows, bias_part)
        backward = (row_weight[:, None] * jnp.exp(scores - row_norm[:, None])).astype(jnp.bfloat16)
        moved = moved + jnp.dot(backward, column_rows, preferred_element_type=jnp.float32)
        column_sums = lax.dynamic_update_slice_in_dim(
            column_sums, jnp.sum(backward.astype(jnp.float32), axis=0), first_row + offset, 0
        )
        return (moved, column_sums)

    return lax.fori_loop(0, length // size, inner, carried)


def shards(particles, log_weight, trans_weight, precision):
    steps_here, rows_here, width = particles.shape
    tm_count = lax.axis_size("tm")
    dom_count = lax.axis_size("dom")
    total_rows = rows_here * dom_count
    tm_place = lax.axis_index("tm")
    is_last = tm_place == tm_count - 1
    weight_full = trans_weight.astype(jnp.float32)
    boundary = from_behind(particles[0], "tm", -1)
    later_sets = [particles[1]] + [boundary]
    later_proj = [project_rows(rows, precision, weight_full) for rows in later_sets]
    biases = []
    for k in range(steps_here):
        predicted = jnp.dot(particles[k], trans_weight.T, preferred_element_type=jnp.float32)
        biases.append(log_weight[k] - 0.5 * jnp.sum(precision * predicted * predicted, axis=1))
    local_bias = jnp.stack(biases)
    full_bias = lax.all_gather(local_bias, "dom", axis=1, tiled=True)
    row_norms = []
    whole = lax.all_gather(particles, "dom", axis=1, tiled=True)
    for k in range(steps_here):
        start_state = (
            jnp.full((rows_here,), -jnp.inf, jnp.float32),
            jnp.zeros((rows_here,), jnp.float32),
        )
        row_top, row_total = make_norm_fold(later_proj[k], full_bias[k], start_state, whole[k], 0)
        row_norms.append(row_top + jnp.log(row_total))
    final_logs = log_weight[steps_here - 1]
    global_top = lax.pmax(jnp.max(final_logs), "dom")
    global_total = lax.psum(jnp.sum(jnp.exp(final_logs - global_top)), "dom")
    final_weights = jnp.exp(final_logs - global_top) / global_total
    carried = (
        jnp.zeros((steps_here, rows_here), jnp.float32),
        jnp.zeros((width, width), jnp.float32),
    )
    for r in range(tm_count):
        if r == 0:
            incoming = jnp.zeros((rows_here,), jnp.float32)
        else:
            incoming = from_behind(carried[0][0], "tm", -1)
        owner = tm_count - 1 - r
        backward_partial_value = jnp.zeros((width, width), jnp.float32)
        outputs = [None] * steps_here
        row_weight = incoming
        for backward_k in range(steps_here - 1, -1, -1):
            column_rows = particles[backward_k]
            backward_start_state = (
                jnp.zeros((rows_here, width), jnp.float32),
                jnp.zeros((total_rows,), jnp.float32),
            )
            moved, column_sums = make_column_fold(
                later_proj[backward_k],
                full_bias[backward_k],
                row_norms[backward_k],
                row_weight,
                backward_start_state,
                whole[backward_k],
                0,
            )
            column_weights = lax.psum_scatter(column_sums, "dom", scatter_dimension=0, tiled=True)
            outer = jnp.dot(
                later_sets[backward_k].astype(jnp.float32).T, moved, precision=exact_mode
            )
            column_float = column_rows.astype(jnp.float32)
            moment = jnp.dot(
                column_float.T * column_weights[None, :], column_float, precision=exact_mode
            )
            backward_partial_value = backward_partial_value + precision[:, None] * (
                outer - jnp.dot(weight_full, moment, precision=exact_mode)
            )
            if backward_k == steps_here - 1:
                column_weights = jnp.where(is_last, final_weights, column_weights)
            outputs[backward_k] = column_weights
            row_weight = column_weights
        is_owner = tm_place == owner
        carried = (
            jnp.where(is_owner, jnp.stack(outputs), carried[0]),
            jnp.where(is_owner, backward_partial_value, carried[1]),
        )
    stacked, partial_value = carried
    score = lax.psum(partial_value, ("dom", "tm"))
    return (stacked * total_rows, score)


MESH = pl.DeviceIdType.MESH
EXTRA = 16
MOST_ROWS = 1024


def nt_dot(a, b):
    return lax.dot_general(a, b, (((1,), (1,)), ((), ())), preferred_element_type=jnp.float32)


def tn_dot(a, b):
    return lax.dot_general(a, b, (((0,), (0,)), ((), ())), preferred_element_type=jnp.float32)


def nn_dot(a, b):
    return jnp.dot(a, b, preferred_element_type=jnp.float32)


def split_three(x):
    high = x.astype(jnp.bfloat16)
    rest = x - high.astype(jnp.float32)
    middle = rest.astype(jnp.bfloat16)
    low = (rest - middle.astype(jnp.float32)).astype(jnp.bfloat16)
    return high, middle, low


def smoother_kernel(
    x_hbm, lw_hbm, w_hbm, p_hbm, smoothed_ref, score_ref,
    lw_held, w_ref, p_ref, held, kernel_rows, stats, inverse_norm, bias, projected, predicted, weights, stage,
    in_sem, send_sem, recv_sem, lw_sem, up_sem,
):
    width = x_hbm.shape[1]
    rows = x_hbm.shape[0] // 2
    unit = 2 * rows
    chips, steps = 8, 4
    total = chips * rows
    half = total // 2
    dom = lax.axis_index("dom")
    tm = lax.axis_index("tm")
    z, side = dom // 2, dom % 2
    across = dom + 1 - 2 * side
    other = 1 - tm

    def slot_of(d, q):
        high, low, turn = d // 2, d % 2, q
        return sum(
            scale * (here + there - 2 * here * there)
            for scale, here, there in ((4, z // 2, high), (2, z % 2, low), (1, side, turn))
        )

    loads = [
        pltpu.make_async_copy(source, target, in_sem.at[i])
        for i, (source, target) in enumerate(
            [(lw_hbm, lw_held.at[0, tm]), (w_hbm, w_ref), (p_hbm, p_ref), (x_hbm, held.at[0, tm, 0:unit])]
        )
    ]
    for load in loads:
        load.start()

    barrier = pltpu.get_barrier_semaphore()

    def signal(sem, to_dom, to_tm):
        pl.semaphore_signal(sem, inc=1, device_id={"dom": to_dom, "tm": to_tm}, device_id_type=MESH)

    for d in range(1, 4):

        @pl.when(z < d)
        def _():
            for q in range(2):
                signal(barrier, 2 * d + q, tm)

    signal(barrier, across, tm)
    signal(barrier, dom, other)

    def piece(source, slot, core, lines, index, to_dom, to_tm):
        return pltpu.make_async_remote_copy(
            src_ref=source,
            dst_ref=held.at[slot, core, lines],
            send_sem=send_sem.at[index],
            recv_sem=recv_sem.at[slot, core],
            device_id={"dom": to_dom, "tm": to_tm},
            device_id_type=MESH,
        )

    body, tail = slice(0, unit), slice(unit, unit + EXTRA)

    def copies(slot, index, to_dom, to_tm):
        lw_copy = pltpu.make_async_remote_copy(
            src_ref=lw_hbm,
            dst_ref=lw_held.at[slot, tm],
            send_sem=send_sem.at[2 * index + 1],
            recv_sem=lw_sem.at[slot, tm],
            device_id={"dom": to_dom, "tm": to_tm},
            device_id_type=MESH,
        )
        return lw_copy, piece(x_hbm, slot, tm, body, 2 * index, to_dom, to_tm)

    def to_chip(d, q):
        return copies(slot_of(d, q), 2 * d + q, 2 * d + q, tm)

    def start_all(pair):
        for copy in pair:
            copy.start()

    pl.semaphore_wait(barrier, 2 + 2 * z)
    for d in range(3):

        @pl.when(z > d)
        def _():
            for q in range(2):
                start_all(to_chip(d, q))

    start_all(copies(1, 8, across, tm))
    start_all(copies(0, 9, dom, other))
    for d in range(3):

        @pl.when(z > d)
        def _():
            for q in range(2):
                signal(up_sem.at[slot_of(d, q)], 2 * d + q, tm)

    for d in range(1, 4):

        @pl.when(z < d)
        def _():
            for q in range(2):
                pl.semaphore_wait(up_sem.at[slot_of(d, q)], 1)
                start_all(to_chip(d, q))

    stage[...] = jnp.zeros_like(stage)

    def pack(slot, core):
        for n, value in enumerate(split_three(lw_held[slot, core])):
            stage[2 * n : 2 * n + 2, 0:rows] = value.astype(jnp.float32)
        held[slot, core, tail, :] = stage[...].astype(jnp.bfloat16)

    for load in loads:
        load.wait()
    pack(0, tm)

    def inside(slot, core):
        return pltpu.make_async_remote_copy(
            src_ref=held.at[slot, core],
            dst_ref=held.at[slot, core],
            send_sem=send_sem.at[20 + slot],
            recv_sem=recv_sem.at[slot, core],
            device_id={"dom": dom, "tm": other},
            device_id_type=MESH,
        )

    def arrive(slot, core):
        pltpu.make_async_remote_copy(
            src_ref=lw_held.at[slot, core],
            dst_ref=lw_held.at[slot, core],
            send_sem=send_sem.at[0],
            recv_sem=lw_sem.at[slot, core],
            device_id={"dom": dom, "tm": other},
            device_id_type=MESH,
        ).wait_recv()
        pack(slot, core)
        piece(held.at[slot, core, body], slot, core, body, 0, dom, other).wait_recv()

    weight = w_ref[...]
    p_row = p_ref[...]
    p_down = jnp.broadcast_to(p_row, (width, width)).T
    scaled = jnp.concatenate(split_three(p_down * weight.astype(jnp.float32)), axis=1)
    line = lax.broadcasted_iota(jnp.int32, (EXTRA, 2 * width), 0)
    which = lax.broadcasted_iota(jnp.int32, (EXTRA, 2 * width), 1) // width
    pick = jnp.where((line < 6) & (line % 2 == which), 1.0, 0.0).astype(jnp.bfloat16)

    def rows_of(t, first, last):
        c, k = t // 2, t % 2
        return held[first:last, c, k * rows : (k + 1) * rows, :].reshape((last - first) * rows, width)

    def prepare(first, last):
        span = slice(first * rows, last * rows)
        for c in range(2):
            for r in range(first, last):
                spread = tn_dot(held[r, c, tail, :], pick)
                for k in range(2):
                    bias[2 * c + k, r * rows : (r + 1) * rows, :] = spread[:rows, k * width : (k + 1) * width]
        for t in range(steps):
            x_t = rows_of(t, first, last)
            if t < steps - 1:
                mean = nt_dot(x_t, weight)
                predicted[t, span, :] = mean
                energy = jnp.sum(p_row * mean * mean, axis=1, keepdims=True)
                bias[t, span, :] = bias[t, span, :] - 0.5 * energy
            if t > 0:
                wide = nn_dot(x_t, scaled)
                projected[t - 1, span, :] = (
                    wide[:, :width] + (wide[:, width : 2 * width] + wide[:, 2 * width :])
                ).astype(jnp.bfloat16)

    def tile(t, j, i):
        columns = rows_of(t, j * 4, j * 4 + 4)
        scores = nt_dot(columns, projected[t, i * half : (i + 1) * half, :])
        scores = scores + jnp.concatenate([bias[t, j * half : (j + 1) * half, :]] * (half // width), axis=1)
        top = jnp.max(scores, axis=0, keepdims=True)
        terms = jnp.exp(scores - top)
        kernel_rows[t, j, :, i * half : (i + 1) * half] = terms.astype(jnp.bfloat16)
        stats[t, 2 * j + i, 0:1, :] = top
        stats[t, 2 * j + i, 1:2, :] = jnp.sum(terms, axis=0, keepdims=True)

    def tall_tile(t):
        scores = nt_dot(rows_of(t, 0, 8), projected[t, half:, :])
        scores = scores + jnp.concatenate([bias[t]] * (half // width), axis=1)
        top = jnp.max(scores, axis=0, keepdims=True)
        terms = jnp.exp(scores - top)
        rounded = terms.astype(jnp.bfloat16)
        sums = (jnp.sum(terms, axis=0, keepdims=True), jnp.zeros_like(top))
        for j in range(2):
            kernel_rows[t, j, :, half:] = rounded[j * half : (j + 1) * half]
            stats[t, 2 * j + 1, 0:1, :] = top
            stats[t, 2 * j + 1, 1:2, :] = sums[j]

    arrive(0, other)
    for slot in (1, 2, 3):
        arrive(slot, tm)
        inside(slot, tm).start()
    for slot in (1, 2, 3):
        inside(slot, other).wait_recv()

    prepare(0, 4)
    for t in range(steps - 1):
        tile(t, 0, 0)

    for slot in range(4, 8):
        arrive(slot, tm)
        inside(slot, tm).start()
    for slot in range(4, 8):
        inside(slot, other).wait_recv()

    prepare(4, 8)

    last = bias[steps - 1]
    last = jnp.exp(last - jnp.max(last, axis=0, keepdims=True))
    weights[steps - 1] = last / jnp.sum(last, axis=0, keepdims=True)

    for t in range(steps - 1):
        tile(t, 1, 0)
        tall_tile(t)

    score = jnp.zeros((width, width), jnp.float32)
    for t in range(steps - 2, -1, -1):
        for i in range(2):
            tops = [stats[t, 2 * j + i, 0:1, :] for j in range(2)]
            top = jnp.maximum(tops[0], tops[1])
            scales = [jnp.exp(tops[j] - top) for j in range(2)]
            norm = sum(scales[j] * stats[t, 2 * j + i, 1:2, :] for j in range(2))
            for j in range(2):
                inverse = scales[j] / norm
                for b in range(half // width):
                    at = i * half + b * width
                    inverse_norm[t, j, at : at + width, :] = jnp.broadcast_to(
                        inverse[:, b * width : (b + 1) * width], (width, width)
                    ).T
    for t in range(steps - 2, -1, -1):
        later = rows_of(t + 1, 0, 8).astype(jnp.float32)
        for j in range(2):
            ratio = weights[t + 1] * inverse_norm[t, j]
            right = jnp.concatenate(
                [(ratio * later).astype(jnp.bfloat16), ratio.astype(jnp.bfloat16)], axis=1
            )
            both = nn_dot(kernel_rows[t, j], right)
            now = both[:, width:]
            weights[t, j * half : (j + 1) * half, :] = now
            span = slice(j * half, (j + 1) * half)
            residual = (both[:, :width] - predicted[t, span, :] * now).astype(jnp.bfloat16)
            score = score + tn_dot(residual, rows_of(t, j * 4, j * 4 + 4))
    score_ref[...] = score * p_down
    for k in range(2):
        own = weights[2 * tm + k, 0:rows, :]
        smoothed_ref[k : k + 1, :] = own.T[0:1, :] * total

    for d in range(4):

        @pl.when(z != d)
        def _():
            for q in range(2):
                for copy in to_chip(d, q):
                    copy.wait_send()

    for pair in (copies(1, 8, across, tm), copies(0, 9, dom, other)):
        for copy in pair:
            copy.wait_send()
    for slot in range(1, 8):
        inside(slot, tm).wait_send()


def hand_over(a_in, b_in, a_out, b_out, sems):
    leaving = [
        pltpu.make_async_copy(a_in, a_out, sems.at[0]),
        pltpu.make_async_copy(b_in, b_out, sems.at[1]),
    ]
    for copy in leaving:
        copy.start()
    for copy in leaving:
        copy.wait()


def fused(particles, log_weight, trans_weight, precision):
    steps_here, rows, width = particles.shape
    chips = 8
    total = chips * rows
    whole = pl.BlockSpec(memory_space=pltpu.VMEM)
    arguments = (
        particles.reshape(steps_here * rows, width), log_weight, trans_weight, precision.reshape(1, width)
    )
    smoothed, score = pl.pallas_call(
        smoother_kernel,
        out_shape=(
            pltpu.VMEM((steps_here, rows), jnp.float32),
            pltpu.VMEM((width, width), jnp.float32),
        ),
        in_specs=[pl.BlockSpec(memory_space=pltpu.HBM)] * 4,
        out_specs=(whole, whole),
        scratch_shapes=[
            pltpu.VMEM((chips, 2, steps_here, rows), jnp.float32),
            pltpu.VMEM((width, width), jnp.bfloat16),
            pltpu.VMEM((1, width), jnp.float32),
            pltpu.VMEM((chips, 2, 2 * rows + EXTRA, width), jnp.bfloat16),
            pltpu.VMEM((3, 2, total // 2, total), jnp.bfloat16),
            pltpu.VMEM((3, 4, 8, total // 2), jnp.float32),
            pltpu.VMEM((3, 2, total, width), jnp.float32),
            pltpu.VMEM((4, total, width), jnp.float32),
            pltpu.VMEM((3, total, width), jnp.bfloat16),
            pltpu.VMEM((3, total, width), jnp.float32),
            pltpu.VMEM((4, total, width), jnp.float32),
            pltpu.VMEM((EXTRA, width), jnp.float32),
            pltpu.SemaphoreType.DMA((4,)),
            pltpu.SemaphoreType.DMA((28,)),
            pltpu.SemaphoreType.DMA((chips, 2)),
            pltpu.SemaphoreType.DMA((chips, 2)),
            pltpu.SemaphoreType.REGULAR((8,)),
        ],
        compiler_params=pltpu.CompilerParams(
            collective_id=0, has_side_effects=True, vmem_limit_bytes=40 * 2**20
        ),
    )(*[pltpu.with_memory_space_constraint(a, pltpu.HBM) for a in arguments])
    return pl.pallas_call(
        hand_over,
        out_shape=(
            jax.ShapeDtypeStruct((steps_here, rows), jnp.float32),
            jax.ShapeDtypeStruct((width, width), jnp.float32),
        ),
        in_specs=[whole] * 2,
        out_specs=(pl.BlockSpec(memory_space=pltpu.HBM),) * 2,
        scratch_shapes=[
            pltpu.SemaphoreType.DMA((2,)),
        ],
        compiler_params=pltpu.CompilerParams(vmem_limit_bytes=40 * 2**20),
    )(smoothed, score)


def plan(particles, log_weight, trans_weight, precision):
    steps_here, rows, width = particles.shape
    n_dom = lax.axis_size("dom")
    total = n_dom * rows
    small = total <= MOST_ROWS and total % (2 * width) == 0 and rows <= width and rows % 16 == 0
    shaped = n_dom == 8 and lax.axis_size("tm") == 2 and steps_here == 2 and width == 128
    if small and shaped:
        return fused(particles, log_weight, trans_weight, precision)
    return shards(particles, log_weight, trans_weight, precision)


def solution(mesh):
    placed = (P("tm", ("seq", "dom"), None), P("tm", ("seq", "dom")), P(), P())
    return jax.shard_map(
        plan,
        mesh=mesh,
        in_specs=placed,
        out_specs=(P("tm", ("seq", "dom")), P("seq", None)),
        check_vma=False,
    )
```

```python
import functools

import jax
import jax.numpy as jnp
from jax import lax
from jax.experimental import pallas as pl
from jax.experimental.pallas import tpu as pltpu
from jax.sharding import PartitionSpec as P

exact_mode = lax.Precision.HIGHEST


def from_behind(x, axis, by):
    size = lax.axis_size(axis)
    pairs = [(i, i + by) for i in range(size) if 0 <= i + by < size]
    return lax.ppermute(x, axis, pairs)


def block_size(length):
    best = 1
    for trial in range(1, min(length, 512) + 1):
        if length % trial == 0:
            best = trial
    return best


def project_rows(rows, precision, weight_full):
    return jnp.dot(rows.astype(jnp.float32) * precision, weight_full, precision=exact_mode).astype(
        jnp.bfloat16
    )


def pair_scores(row_proj, column_rows, column_bias):
    return (
        jnp.einsum("id,jd->ij", row_proj, column_rows, preferred_element_type=jnp.float32)
        + column_bias[None, :]
    )


def make_norm_fold(row_proj, bias_row, carried, block_in, first_row):
    length = block_in.shape[0]
    size = block_size(length)

    def inner(position, state):
        row_top, row_total = state
        offset = position * size
        column_rows = lax.dynamic_slice_in_dim(block_in, offset, size, 0)
        bias_part = lax.dynamic_slice_in_dim(bias_row, first_row + offset, size, 0)
        scores = pair_scores(row_proj, column_rows, bias_part)
        new_top = jnp.maximum(row_top, jnp.max(scores, axis=1))
        row_total = row_total * jnp.exp(row_top - new_top) + jnp.sum(
            jnp.exp(scores - new_top[:, None]), axis=1
        )
        return (new_top, row_total)

    return lax.fori_loop(0, length // size, inner, carried)


def make_column_fold(row_proj, bias_row, row_norm, row_weight, carried, block_in, first_row):
    length = block_in.shape[0]
    size = block_size(length)

    def inner(position, state):
        moved, column_sums = state
        offset = position * size
        column_rows = lax.dynamic_slice_in_dim(block_in, offset, size, 0)
        bias_part = lax.dynamic_slice_in_dim(bias_row, first_row + offset, size, 0)
        scores = pair_scores(row_proj, column_rows, bias_part)
        backward = (row_weight[:, None] * jnp.exp(scores - row_norm[:, None])).astype(jnp.bfloat16)
        moved = moved + jnp.dot(backward, column_rows, preferred_element_type=jnp.float32)
        column_sums = lax.dynamic_update_slice_in_dim(
            column_sums, jnp.sum(backward.astype(jnp.float32), axis=0), first_row + offset, 0
        )
        return (moved, column_sums)

    return lax.fori_loop(0, length // size, inner, carried)


def shards(particles, log_weight, trans_weight, precision):
    steps_here, rows_here, width = particles.shape
    tm_count = lax.axis_size("tm")
    dom_count = lax.axis_size("dom")
    total_rows = rows_here * dom_count
    tm_place = lax.axis_index("tm")
    is_last = tm_place == tm_count - 1
    weight_full = trans_weight.astype(jnp.float32)
    boundary = from_behind(particles[0], "tm", -1)
    later_sets = [particles[1]] + [boundary]
    later_proj = [project_rows(rows, precision, weight_full) for rows in later_sets]
    biases = []
    for k in range(steps_here):
        predicted = jnp.dot(particles[k], trans_weight.T, preferred_element_type=jnp.float32)
        biases.append(log_weight[k] - 0.5 * jnp.sum(precision * predicted * predicted, axis=1))
    local_bias = jnp.stack(biases)
    full_bias = lax.all_gather(local_bias, "dom", axis=1, tiled=True)
    row_norms = []
    whole = lax.all_gather(particles, "dom", axis=1, tiled=True)
    for k in range(steps_here):
        start_state = (
            jnp.full((rows_here,), -jnp.inf, jnp.float32),
            jnp.zeros((rows_here,), jnp.float32),
        )
        row_top, row_total = make_norm_fold(later_proj[k], full_bias[k], start_state, whole[k], 0)
        row_norms.append(row_top + jnp.log(row_total))
    final_logs = log_weight[steps_here - 1]
    global_top = lax.pmax(jnp.max(final_logs), "dom")
    global_total = lax.psum(jnp.sum(jnp.exp(final_logs - global_top)), "dom")
    final_weights = jnp.exp(final_logs - global_top) / global_total
    carried = (
        jnp.zeros((steps_here, rows_here), jnp.float32),
        jnp.zeros((width, width), jnp.float32),
    )
    for r in range(tm_count):
        if r == 0:
            incoming = jnp.zeros((rows_here,), jnp.float32)
        else:
            incoming = from_behind(carried[0][0], "tm", -1)
        owner = tm_count - 1 - r
        backward_partial_value = jnp.zeros((width, width), jnp.float32)
        outputs = [None] * steps_here
        row_weight = incoming
        for backward_k in range(steps_here - 1, -1, -1):
            column_rows = particles[backward_k]
            backward_start_state = (
                jnp.zeros((rows_here, width), jnp.float32),
                jnp.zeros((total_rows,), jnp.float32),
            )
            moved, column_sums = make_column_fold(
                later_proj[backward_k],
                full_bias[backward_k],
                row_norms[backward_k],
                row_weight,
                backward_start_state,
                whole[backward_k],
                0,
            )
            column_weights = lax.psum_scatter(column_sums, "dom", scatter_dimension=0, tiled=True)
            outer = jnp.dot(
                later_sets[backward_k].astype(jnp.float32).T, moved, precision=exact_mode
            )
            column_float = column_rows.astype(jnp.float32)
            moment = jnp.dot(
                column_float.T * column_weights[None, :], column_float, precision=exact_mode
            )
            backward_partial_value = backward_partial_value + precision[:, None] * (
                outer - jnp.dot(weight_full, moment, precision=exact_mode)
            )
            if backward_k == steps_here - 1:
                column_weights = jnp.where(is_last, final_weights, column_weights)
            outputs[backward_k] = column_weights
            row_weight = column_weights
        is_owner = tm_place == owner
        carried = (
            jnp.where(is_owner, jnp.stack(outputs), carried[0]),
            jnp.where(is_owner, backward_partial_value, carried[1]),
        )
    stacked, partial_value = carried
    score = lax.psum(partial_value, ("dom", "tm"))
    return (stacked * total_rows, score)


MESH = pl.DeviceIdType.MESH
EXTRA = 16
CHIPS = 8
MOST_ROWS = 1024


def nt_dot(a, b):
    return lax.dot_general(a, b, (((1,), (1,)), ((), ())), preferred_element_type=jnp.float32)


def tn_dot(a, b):
    return lax.dot_general(a, b, (((0,), (0,)), ((), ())), preferred_element_type=jnp.float32)


def nn_dot(a, b):
    return jnp.dot(a, b, preferred_element_type=jnp.float32)


def split_three(x):
    high = x.astype(jnp.bfloat16)
    rest = x - high.astype(jnp.float32)
    middle = rest.astype(jnp.bfloat16)
    low = (rest - middle.astype(jnp.float32)).astype(jnp.bfloat16)
    return high, middle, low


def smoother_kernel(
    x_hbm, lw_hbm, w_hbm, p_hbm, smoothed_ref, score_ref,
    lw_held, w_ref, p_ref, held, middle_rows, kernel_rows, stats, inverse_norm, bias, projected, predicted,
    weights, stage, lean, score_mine, score_theirs,
    in_sem, send_sem, lw_send_sem, inside_send_sem, recv_sem, lw_sem, inside_sem, late_sem, up_sem,
):
    width = x_hbm.shape[1]
    rows = x_hbm.shape[0] // 2
    total = CHIPS * rows
    half = total // 2
    dom = lax.axis_index("dom")
    tm = lax.axis_index("tm")
    z, side = dom // 2, dom % 2
    across = dom + 1 - 2 * side
    other = 1 - tm

    def slot_of(d, q):
        high, low = d // 2, d % 2
        return sum(
            scale * (here + there - 2 * here * there)
            for scale, here, there in ((4, z // 2, high), (2, z % 2, low), (1, side, q))
        )

    loads = [
        pltpu.make_async_copy(source, target, in_sem.at[i])
        for i, (source, target) in enumerate(
            [(lw_hbm, lw_held.at[0]), (w_hbm, w_ref), (p_hbm, p_ref), (x_hbm, held.at[0])]
        )
    ]
    for load in loads:
        load.start()

    barrier = pltpu.get_barrier_semaphore()

    def signal(sem, to_dom, to_tm):
        pl.semaphore_signal(sem, inc=1, device_id={"dom": to_dom, "tm": to_tm}, device_id_type=MESH)

    for d in range(1, 4):

        @pl.when(z < d)
        def _():
            for q in range(2):
                signal(barrier, 2 * d + q, tm)

    signal(barrier, across, tm)
    signal(barrier, dom, other)

    def remote(source, target, send, recv, to_dom, to_tm):
        return pltpu.make_async_remote_copy(
            src_ref=source,
            dst_ref=target,
            send_sem=send,
            recv_sem=recv,
            device_id={"dom": to_dom, "tm": to_tm},
            device_id_type=MESH,
        )

    def own(slot, to_dom):
        return (
            remote(lw_hbm, lw_held.at[slot], lw_send_sem.at[slot], lw_sem.at[slot], to_dom, tm),
            remote(x_hbm, held.at[slot], send_sem.at[slot], recv_sem.at[slot], to_dom, tm),
        )

    def start_own(slot, to_dom):
        for copy in own(slot, to_dom):
            copy.start()

    def middle(slot):
        source = x_hbm if slot == 0 else held.at[slot]
        return remote(
            source.at[0:rows], middle_rows.at[slot], inside_send_sem.at[slot], inside_sem.at[slot], dom, other
        )

    lean_copy = remote(lean, lean, inside_send_sem.at[CHIPS], late_sem.at[0], dom, other)
    score_copy = remote(score_mine, score_theirs, inside_send_sem.at[CHIPS + 1], late_sem.at[1], dom, other)

    pl.semaphore_wait(barrier, 2 + 2 * z)
    for d in range(3):

        @pl.when(z > d)
        def _():
            for q in range(2):
                start_own(slot_of(d, q), 2 * d + q)

    start_own(1, across)
    for d in range(3):

        @pl.when(z > d)
        def _():
            for q in range(2):
                signal(up_sem.at[slot_of(d, q)], 2 * d + q, tm)

    for d in range(1, 4):

        @pl.when(z < d)
        def _():
            for q in range(2):
                pl.semaphore_wait(up_sem.at[slot_of(d, q)], 1)
                start_own(slot_of(d, q), 2 * d + q)

    stage[...] = jnp.zeros_like(stage)
    for load in loads:
        load.wait()

    def arrive(slot):
        for copy in own(slot, across):
            copy.wait_recv()

    weight = w_ref[...]
    p_row = p_ref[...]
    p_down = jnp.broadcast_to(p_row, (width, width)).T
    scaled = jnp.concatenate(split_three(p_down * weight.astype(jnp.float32)), axis=1)
    line = lax.broadcasted_iota(jnp.int32, (EXTRA, 2 * width), 0)
    which = lax.broadcasted_iota(jnp.int32, (EXTRA, 2 * width), 1) // width
    pick = jnp.where((line < 6) & (line % 2 == which), 1.0, 0.0).astype(jnp.bfloat16)

    def flat(block):
        return block.reshape(block.shape[0] * rows, width)

    def columns_of(e, first, last):
        return flat(held[first:last, e * rows : (e + 1) * rows, :])

    def rows_of(e, first, last):
        return flat(middle_rows[first:last] if e else held[first:last, rows:, :])

    def spread_logs(first, last):
        for r in range(first, last):
            for n, value in enumerate(split_three(lw_held[r])):
                stage[r, 2 * n : 2 * n + 2, 0:rows] = value.astype(jnp.float32)
            spread = tn_dot(stage[r].astype(jnp.bfloat16), pick)
            for e in range(2):
                bias[e, r * rows : (r + 1) * rows, :] = spread[:rows, e * width : (e + 1) * width]

    def prepare(e, first, last):
        span = slice(first * rows, last * rows)
        mean = nt_dot(columns_of(e, first, last), weight)
        predicted[e, span, :] = mean
        energy = jnp.sum(p_row * mean * mean, axis=1, keepdims=True)
        bias[e, span, :] = bias[e, span, :] - 0.5 * energy
        wide = nn_dot(rows_of(e, first, last), scaled)
        projected[e, span, :] = (
            wide[:, :width] + (wide[:, width : 2 * width] + wide[:, 2 * width :])
        ).astype(jnp.bfloat16)

    def tile(e, j, i):
        columns = columns_of(e, j * 4, j * 4 + 4)
        scores = nt_dot(columns, projected[e, i * half : (i + 1) * half, :])
        scores = scores + jnp.concatenate([bias[e, j * half : (j + 1) * half, :]] * (half // width), axis=1)
        top = jnp.max(scores, axis=0, keepdims=True)
        terms = jnp.exp(scores - top)
        kernel_rows[e, j, :, i * half : (i + 1) * half] = terms.astype(jnp.bfloat16)
        stats[e, 2 * j + i, 0:1, :] = top
        stats[e, 2 * j + i, 1:2, :] = jnp.sum(terms, axis=0, keepdims=True)

    def tall_tile(e):
        scores = nt_dot(columns_of(e, 0, CHIPS), projected[e, half:, :])
        scores = scores + jnp.concatenate([bias[e]] * (half // width), axis=1)
        top = jnp.max(scores, axis=0, keepdims=True)
        terms = jnp.exp(scores - top)
        rounded = terms.astype(jnp.bfloat16)
        sums = (jnp.sum(terms, axis=0, keepdims=True), jnp.zeros_like(top))
        for j in range(2):
            kernel_rows[e, j, :, half:] = rounded[j * half : (j + 1) * half]
            stats[e, 2 * j + 1, 0:1, :] = top
            stats[e, 2 * j + 1, 1:2, :] = sums[j]

    def turn(row):
        return jnp.broadcast_to(row, (width, width)).T

    def normalize(e):
        for i in range(2):
            tops = [stats[e, 2 * j + i, 0:1, :] for j in range(2)]
            top = jnp.maximum(tops[0], tops[1])
            scales = [jnp.exp(tops[j] - top) for j in range(2)]
            norm = sum(scales[j] * stats[e, 2 * j + i, 1:2, :] for j in range(2))
            for j in range(2):
                inverse = scales[j] / norm
                for b in range(half // width):
                    at = i * half + b * width
                    inverse_norm[e, j, at : at + width, :] = turn(inverse[:, b * width : (b + 1) * width])

    def step_back(e, came, gives):
        later = rows_of(e, 0, CHIPS).astype(jnp.float32)
        moved = []
        for j in range(2):
            ratio = weights[came] * inverse_norm[e, j]
            right = jnp.concatenate(
                [(ratio * later).astype(jnp.bfloat16), ratio.astype(jnp.bfloat16)], axis=1
            )
            both = nn_dot(kernel_rows[e, j], right)
            weights[gives, j * half : (j + 1) * half, :] = both[:, width:]
            moved.append(both[:, :width])
        return moved

    def gradient(e, moved, gives):
        part = jnp.zeros((width, width), jnp.float32)
        for j in range(2):
            span = slice(j * half, (j + 1) * half)
            residual = (moved[j] - predicted[e, span, :] * weights[gives, span, :]).astype(jnp.bfloat16)
            part = part + tn_dot(residual, columns_of(e, j * 4, j * 4 + 4))
        return part

    @pl.when(tm == 1)
    def _():
        middle(0).start()

    for slot in range(1, 4):
        arrive(slot)

        @pl.when(tm == 1)
        def _():
            middle(slot).start()

    spread_logs(0, 4)
    prepare(0, 0, 4)
    tile(0, 0, 0)

    @pl.when(tm == 0)
    def _():
        for slot in range(4):
            middle(slot).wait_recv()
        prepare(1, 0, 4)
        tile(1, 0, 0)

    for slot in range(4, CHIPS):
        arrive(slot)

        @pl.when(tm == 1)
        def _():
            middle(slot).start()

    spread_logs(4, CHIPS)
    prepare(0, 4, CHIPS)
    tile(0, 1, 0)
    tall_tile(0)
    normalize(0)

    @pl.when(tm == 1)
    def _():
        last = jnp.exp(bias[1] - jnp.max(bias[1], axis=0, keepdims=True))
        weights[1] = last / jnp.sum(last, axis=0, keepdims=True)
        moved = step_back(0, 1, 0)
        for b in range(total // width):
            lean[b : b + 1, :] = weights[0, b * width : (b + 1) * width, :].T[0:1, :]
        lean_copy.start()
        score_mine[...] = gradient(0, moved, 0)

    @pl.when(tm == 0)
    def _():
        for slot in range(4, CHIPS):
            middle(slot).wait_recv()
        prepare(1, 4, CHIPS)
        tile(1, 1, 0)
        tall_tile(1)
        normalize(1)
        lean_copy.wait_recv()
        for b in range(total // width):
            weights[2, b * width : (b + 1) * width, :] = turn(lean[b : b + 1, :])
        moved = step_back(1, 2, 1)
        part = gradient(1, moved, 1)
        moved = step_back(0, 1, 0)
        score_mine[...] = part + gradient(0, moved, 0)

    score_copy.start()
    for k in range(2):
        smoothed_ref[k : k + 1, :] = weights[k, 0:rows, :].T[0:1, :] * total
    score_copy.wait_recv()
    score_ref[...] = (score_mine[...] + score_theirs[...]) * p_down

    for d in range(4):

        @pl.when(z != d)
        def _():
            for q in range(2):
                for copy in own(slot_of(d, q), 2 * d + q):
                    copy.wait_send()

    for copy in own(1, across):
        copy.wait_send()
    score_copy.wait_send()

    @pl.when(tm == 1)
    def _():
        for slot in range(CHIPS):
            middle(slot).wait_send()
        lean_copy.wait_send()


def hand_over(a_in, b_in, a_out, b_out, sems):
    leaving = [
        pltpu.make_async_copy(a_in, a_out, sems.at[0]),
        pltpu.make_async_copy(b_in, b_out, sems.at[1]),
    ]
    for copy in leaving:
        copy.start()
    for copy in leaving:
        copy.wait()


def fused(particles, log_weight, trans_weight, precision):
    steps_here, rows, width = particles.shape
    total = CHIPS * rows
    whole = pl.BlockSpec(memory_space=pltpu.VMEM)
    arguments = (
        particles.reshape(steps_here * rows, width), log_weight, trans_weight, precision.reshape(1, width)
    )
    smoothed, score = pl.pallas_call(
        smoother_kernel,
        out_shape=(
            pltpu.VMEM((steps_here, rows), jnp.float32),
            pltpu.VMEM((width, width), jnp.float32),
        ),
        in_specs=[pl.BlockSpec(memory_space=pltpu.HBM)] * 4,
        out_specs=(whole, whole),
        scratch_shapes=[
            pltpu.VMEM((CHIPS, steps_here, rows), jnp.float32),
            pltpu.VMEM((width, width), jnp.bfloat16),
            pltpu.VMEM((1, width), jnp.float32),
            pltpu.VMEM((CHIPS, 2 * rows, width), jnp.bfloat16),
            pltpu.VMEM((CHIPS, rows, width), jnp.bfloat16),
            pltpu.VMEM((2, 2, total // 2, total), jnp.bfloat16),
            pltpu.VMEM((2, 4, 8, total // 2), jnp.float32),
            pltpu.VMEM((2, 2, total, width), jnp.float32),
            pltpu.VMEM((2, total, width), jnp.float32),
            pltpu.VMEM((2, total, width), jnp.bfloat16),
            pltpu.VMEM((2, total, width), jnp.float32),
            pltpu.VMEM((3, total, width), jnp.float32),
            pltpu.VMEM((CHIPS, EXTRA, width), jnp.float32),
            pltpu.VMEM((8, width), jnp.float32),
            pltpu.VMEM((width, width), jnp.float32),
            pltpu.VMEM((width, width), jnp.float32),
            pltpu.SemaphoreType.DMA((4,)),
            pltpu.SemaphoreType.DMA((CHIPS,)),
            pltpu.SemaphoreType.DMA((CHIPS,)),
            pltpu.SemaphoreType.DMA((CHIPS + 2,)),
            pltpu.SemaphoreType.DMA((CHIPS,)),
            pltpu.SemaphoreType.DMA((CHIPS,)),
            pltpu.SemaphoreType.DMA((CHIPS,)),
            pltpu.SemaphoreType.DMA((2,)),
            pltpu.SemaphoreType.REGULAR((CHIPS,)),
        ],
        compiler_params=pltpu.CompilerParams(
            collective_id=0, has_side_effects=True, vmem_limit_bytes=40 * 2**20
        ),
    )(*[pltpu.with_memory_space_constraint(a, pltpu.HBM) for a in arguments])
    return pl.pallas_call(
        hand_over,
        out_shape=(
            jax.ShapeDtypeStruct((steps_here, rows), jnp.float32),
            jax.ShapeDtypeStruct((width, width), jnp.float32),
        ),
        in_specs=[whole] * 2,
        out_specs=(pl.BlockSpec(memory_space=pltpu.HBM),) * 2,
        scratch_shapes=[
            pltpu.SemaphoreType.DMA((2,)),
        ],
        compiler_params=pltpu.CompilerParams(vmem_limit_bytes=40 * 2**20),
    )(smoothed, score)


def plan(particles, log_weight, trans_weight, precision):
    steps_here, rows, width = particles.shape
    n_dom = lax.axis_size("dom")
    total = n_dom * rows
    small = total <= MOST_ROWS and total % (2 * width) == 0 and rows <= width and rows % 16 == 0
    shaped = n_dom == 8 and lax.axis_size("tm") == 2 and steps_here == 2 and width == 128
    if small and shaped:
        return fused(particles, log_weight, trans_weight, precision)
    return shards(particles, log_weight, trans_weight, precision)


def solution(mesh):
    placed = (P("tm", ("seq", "dom"), None), P("tm", ("seq", "dom")), P(), P())
    return jax.shard_map(
        plan,
        mesh=mesh,
        in_specs=placed,
        out_specs=(P("tm", ("seq", "dom")), P("seq", None)),
        check_vma=False,
    )
```

```python
import functools

import jax
import jax.numpy as jnp
from jax import lax
from jax.experimental import pallas as pl
from jax.experimental.pallas import tpu as pltpu
from jax.sharding import PartitionSpec as P

exact_mode = lax.Precision.HIGHEST


def from_behind(x, axis, by):
    size = lax.axis_size(axis)
    pairs = [(i, i + by) for i in range(size) if 0 <= i + by < size]
    return lax.ppermute(x, axis, pairs)


def block_size(length):
    best = 1
    for trial in range(1, min(length, 512) + 1):
        if length % trial == 0:
            best = trial
    return best


def project_rows(rows, precision, weight_full):
    return jnp.dot(rows.astype(jnp.float32) * precision, weight_full, precision=exact_mode).astype(
        jnp.bfloat16
    )


def pair_scores(row_proj, column_rows, column_bias):
    return (
        jnp.einsum("id,jd->ij", row_proj, column_rows, preferred_element_type=jnp.float32)
        + column_bias[None, :]
    )


def make_norm_fold(row_proj, bias_row, carried, block_in, first_row):
    length = block_in.shape[0]
    size = block_size(length)

    def inner(position, state):
        row_top, row_total = state
        offset = position * size
        column_rows = lax.dynamic_slice_in_dim(block_in, offset, size, 0)
        bias_part = lax.dynamic_slice_in_dim(bias_row, first_row + offset, size, 0)
        scores = pair_scores(row_proj, column_rows, bias_part)
        new_top = jnp.maximum(row_top, jnp.max(scores, axis=1))
        row_total = row_total * jnp.exp(row_top - new_top) + jnp.sum(
            jnp.exp(scores - new_top[:, None]), axis=1
        )
        return (new_top, row_total)

    return lax.fori_loop(0, length // size, inner, carried)


def make_column_fold(row_proj, bias_row, row_norm, row_weight, carried, block_in, first_row):
    length = block_in.shape[0]
    size = block_size(length)

    def inner(position, state):
        moved, column_sums = state
        offset = position * size
        column_rows = lax.dynamic_slice_in_dim(block_in, offset, size, 0)
        bias_part = lax.dynamic_slice_in_dim(bias_row, first_row + offset, size, 0)
        scores = pair_scores(row_proj, column_rows, bias_part)
        backward = (row_weight[:, None] * jnp.exp(scores - row_norm[:, None])).astype(jnp.bfloat16)
        moved = moved + jnp.dot(backward, column_rows, preferred_element_type=jnp.float32)
        column_sums = lax.dynamic_update_slice_in_dim(
            column_sums, jnp.sum(backward.astype(jnp.float32), axis=0), first_row + offset, 0
        )
        return (moved, column_sums)

    return lax.fori_loop(0, length // size, inner, carried)


def shards(particles, log_weight, trans_weight, precision):
    steps_here, rows_here, width = particles.shape
    tm_count = lax.axis_size("tm")
    dom_count = lax.axis_size("dom")
    total_rows = rows_here * dom_count
    tm_place = lax.axis_index("tm")
    is_last = tm_place == tm_count - 1
    weight_full = trans_weight.astype(jnp.float32)
    boundary = from_behind(particles[0], "tm", -1)
    later_sets = [particles[1]] + [boundary]
    later_proj = [project_rows(rows, precision, weight_full) for rows in later_sets]
    biases = []
    for k in range(steps_here):
        predicted = jnp.dot(particles[k], trans_weight.T, preferred_element_type=jnp.float32)
        biases.append(log_weight[k] - 0.5 * jnp.sum(precision * predicted * predicted, axis=1))
    local_bias = jnp.stack(biases)
    full_bias = lax.all_gather(local_bias, "dom", axis=1, tiled=True)
    row_norms = []
    whole = lax.all_gather(particles, "dom", axis=1, tiled=True)
    for k in range(steps_here):
        start_state = (
            jnp.full((rows_here,), -jnp.inf, jnp.float32),
            jnp.zeros((rows_here,), jnp.float32),
        )
        row_top, row_total = make_norm_fold(later_proj[k], full_bias[k], start_state, whole[k], 0)
        row_norms.append(row_top + jnp.log(row_total))
    final_logs = log_weight[steps_here - 1]
    global_top = lax.pmax(jnp.max(final_logs), "dom")
    global_total = lax.psum(jnp.sum(jnp.exp(final_logs - global_top)), "dom")
    final_weights = jnp.exp(final_logs - global_top) / global_total
    carried = (
        jnp.zeros((steps_here, rows_here), jnp.float32),
        jnp.zeros((width, width), jnp.float32),
    )
    for r in range(tm_count):
        if r == 0:
            incoming = jnp.zeros((rows_here,), jnp.float32)
        else:
            incoming = from_behind(carried[0][0], "tm", -1)
        owner = tm_count - 1 - r
        backward_partial_value = jnp.zeros((width, width), jnp.float32)
        outputs = [None] * steps_here
        row_weight = incoming
        for backward_k in range(steps_here - 1, -1, -1):
            column_rows = particles[backward_k]
            backward_start_state = (
                jnp.zeros((rows_here, width), jnp.float32),
                jnp.zeros((total_rows,), jnp.float32),
            )
            moved, column_sums = make_column_fold(
                later_proj[backward_k],
                full_bias[backward_k],
                row_norms[backward_k],
                row_weight,
                backward_start_state,
                whole[backward_k],
                0,
            )
            column_weights = lax.psum_scatter(column_sums, "dom", scatter_dimension=0, tiled=True)
            outer = jnp.dot(
                later_sets[backward_k].astype(jnp.float32).T, moved, precision=exact_mode
            )
            column_float = column_rows.astype(jnp.float32)
            moment = jnp.dot(
                column_float.T * column_weights[None, :], column_float, precision=exact_mode
            )
            backward_partial_value = backward_partial_value + precision[:, None] * (
                outer - jnp.dot(weight_full, moment, precision=exact_mode)
            )
            if backward_k == steps_here - 1:
                column_weights = jnp.where(is_last, final_weights, column_weights)
            outputs[backward_k] = column_weights
            row_weight = column_weights
        is_owner = tm_place == owner
        carried = (
            jnp.where(is_owner, jnp.stack(outputs), carried[0]),
            jnp.where(is_owner, backward_partial_value, carried[1]),
        )
    stacked, partial_value = carried
    score = lax.psum(partial_value, ("dom", "tm"))
    return (stacked * total_rows, score)


MESH = pl.DeviceIdType.MESH
EXTRA = 16
CHIPS = 8
MOST_ROWS = 1024


def nt_dot(a, b):
    return lax.dot_general(a, b, (((1,), (1,)), ((), ())), preferred_element_type=jnp.float32)


def tn_dot(a, b):
    return lax.dot_general(a, b, (((0,), (0,)), ((), ())), preferred_element_type=jnp.float32)


def nn_dot(a, b):
    return jnp.dot(a, b, preferred_element_type=jnp.float32)


def split_three(x):
    high = x.astype(jnp.bfloat16)
    rest = x - high.astype(jnp.float32)
    middle = rest.astype(jnp.bfloat16)
    low = (rest - middle.astype(jnp.float32)).astype(jnp.bfloat16)
    return high, middle, low


def smoother_kernel(
    x_hbm, lw_hbm, w_hbm, p_hbm, smoothed_ref, score_ref,
    lw_held, w_ref, p_ref, held, middle_rows, kernel_rows, stats, inverse_norm, bias, projected, predicted,
    weights, stage, lean, score_mine, score_theirs,
    in_sem, send_sem, lw_send_sem, inside_send_sem, recv_sem, lw_sem, inside_sem, late_sem, up_sem,
):
    width = x_hbm.shape[1]
    rows = x_hbm.shape[0] // 2
    total = CHIPS * rows
    half = total // 2
    dom = lax.axis_index("dom")
    tm = lax.axis_index("tm")
    z, side = dom // 2, dom % 2
    across = dom + 1 - 2 * side
    other = 1 - tm

    def slot_of(d, q):
        high, low = d // 2, d % 2
        return sum(
            scale * (here + there - 2 * here * there)
            for scale, here, there in ((4, z // 2, high), (2, z % 2, low), (1, side, q))
        )

    loads = [
        pltpu.make_async_copy(source, target, in_sem.at[i])
        for i, (source, target) in enumerate(
            [(lw_hbm, lw_held.at[0]), (w_hbm, w_ref), (p_hbm, p_ref), (x_hbm, held.at[0])]
        )
    ]
    barrier = pltpu.get_barrier_semaphore()

    def signal(sem, to_dom, to_tm):
        pl.semaphore_signal(sem, inc=1, device_id={"dom": to_dom, "tm": to_tm}, device_id_type=MESH)

    for d in range(1, 4):

        @pl.when(z < d)
        def _():
            for q in range(2):
                signal(barrier, 2 * d + q, tm)

    signal(barrier, across, tm)
    signal(barrier, dom, other)

    def remote(source, target, send, recv, to_dom, to_tm):
        return pltpu.make_async_remote_copy(
            src_ref=source,
            dst_ref=target,
            send_sem=send,
            recv_sem=recv,
            device_id={"dom": to_dom, "tm": to_tm},
            device_id_type=MESH,
        )

    def own(slot, to_dom):
        return (
            remote(lw_hbm, lw_held.at[slot], lw_send_sem.at[slot], lw_sem.at[slot], to_dom, tm),
            remote(x_hbm, held.at[slot], send_sem.at[slot], recv_sem.at[slot], to_dom, tm),
        )

    def start_own(d, q):
        def start():
            for copy in own(slot_of(d, q), 2 * d + q):
                copy.start()

        pl.when(sends_to(d, q))(start)

    def sends_to(d, q):
        same_half = z // 2 == d // 2
        return jnp.logical_or(jnp.logical_or(same_half, tm == 0), side == q)

    def sideways(slot):
        return (
            remote(
                lw_held.at[slot], lw_held.at[slot + 1], lw_send_sem.at[slot + 1], lw_sem.at[slot + 1], across, tm
            ),
            remote(held.at[slot], held.at[slot + 1], send_sem.at[slot + 1], recv_sem.at[slot + 1], across, tm),
        )

    def middle(slot):
        source = x_hbm if slot == 0 else held.at[slot]
        return remote(
            source.at[0:rows], middle_rows.at[slot], inside_send_sem.at[slot], inside_sem.at[slot], dom, other
        )

    lean_copy = remote(lean, lean, inside_send_sem.at[CHIPS], late_sem.at[0], dom, other)
    score_copy = remote(score_mine, score_theirs, inside_send_sem.at[CHIPS + 1], late_sem.at[1], dom, other)

    pl.semaphore_wait(barrier, 2 + 2 * z)
    for d in range(3):

        @pl.when(z > d)
        def _():
            for q in range(2):
                signal(up_sem.at[slot_of(d, q)], 2 * d + q, tm)

    for d in range(3):

        @pl.when(z > d)
        def _():
            for q in range(2):
                start_own(d, q)

    for copy in own(1, across):
        copy.start()

    @pl.when(tm == 1)
    def _():
        middle(0).start()

    for load in loads:
        load.start()

    for d in range(1, 4):

        @pl.when(z < d)
        def _():
            for q in range(2):
                pl.semaphore_wait(up_sem.at[slot_of(d, q)], 1)
                start_own(d, q)

    stage[...] = jnp.zeros_like(stage)
    for load in loads:
        load.wait()

    def arrive(slot):
        for copy in own(slot, across):
            copy.wait_recv()

    weight = w_ref[...]
    p_row = p_ref[...]
    p_down = jnp.broadcast_to(p_row, (width, width)).T
    scaled = jnp.concatenate(split_three(p_down * weight.astype(jnp.float32)), axis=1)
    line = lax.broadcasted_iota(jnp.int32, (EXTRA, 2 * width), 0)
    which = lax.broadcasted_iota(jnp.int32, (EXTRA, 2 * width), 1) // width
    pick = jnp.where((line < 6) & (line % 2 == which), 1.0, 0.0).astype(jnp.bfloat16)

    def flat(block):
        return block.reshape(block.shape[0] * rows, width)

    def columns_of(e, first, last):
        return flat(held[first:last, e * rows : (e + 1) * rows, :])

    def rows_of(e, first, last):
        return flat(middle_rows[first:last] if e else held[first:last, rows:, :])

    def spread_logs(first, last):
        for r in range(first, last):
            for n, value in enumerate(split_three(lw_held[r])):
                stage[r, 2 * n : 2 * n + 2, 0:rows] = value.astype(jnp.float32)
            spread = tn_dot(stage[r].astype(jnp.bfloat16), pick)
            for e in range(2):
                bias[e, r * rows : (r + 1) * rows, :] = spread[:rows, e * width : (e + 1) * width]

    def prepare(e, first, last):
        span = slice(first * rows, last * rows)
        mean = nt_dot(columns_of(e, first, last), weight)
        predicted[e, span, :] = mean
        energy = jnp.sum(p_row * mean * mean, axis=1, keepdims=True)
        bias[e, span, :] = bias[e, span, :] - 0.5 * energy
        wide = nn_dot(rows_of(e, first, last), scaled)
        projected[e, span, :] = (
            wide[:, :width] + (wide[:, width : 2 * width] + wide[:, 2 * width :])
        ).astype(jnp.bfloat16)

    def tile(e, j, i):
        columns = columns_of(e, j * 4, j * 4 + 4)
        scores = nt_dot(columns, projected[e, i * half : (i + 1) * half, :])
        scores = scores + jnp.concatenate([bias[e, j * half : (j + 1) * half, :]] * (half // width), axis=1)
        top = jnp.max(scores, axis=0, keepdims=True)
        terms = jnp.exp(scores - top)
        kernel_rows[e, j, :, i * half : (i + 1) * half] = terms.astype(jnp.bfloat16)
        stats[e, 2 * j + i, 0:1, :] = top
        stats[e, 2 * j + i, 1:2, :] = jnp.sum(terms, axis=0, keepdims=True)

    def tall_tile(e):
        scores = nt_dot(columns_of(e, 0, CHIPS), projected[e, half:, :])
        scores = scores + jnp.concatenate([bias[e]] * (half // width), axis=1)
        top = jnp.max(scores, axis=0, keepdims=True)
        terms = jnp.exp(scores - top)
        rounded = terms.astype(jnp.bfloat16)
        sums = (jnp.sum(terms, axis=0, keepdims=True), jnp.zeros_like(top))
        for j in range(2):
            kernel_rows[e, j, :, half:] = rounded[j * half : (j + 1) * half]
            stats[e, 2 * j + 1, 0:1, :] = top
            stats[e, 2 * j + 1, 1:2, :] = sums[j]

    def turn(row):
        return jnp.broadcast_to(row, (width, width)).T

    def normalize(e):
        for i in range(2):
            tops = [stats[e, 2 * j + i, 0:1, :] for j in range(2)]
            top = jnp.maximum(tops[0], tops[1])
            scales = [jnp.exp(tops[j] - top) for j in range(2)]
            norm = sum(scales[j] * stats[e, 2 * j + i, 1:2, :] for j in range(2))
            for j in range(2):
                inverse = scales[j] / norm
                for b in range(half // width):
                    at = i * half + b * width
                    inverse_norm[e, j, at : at + width, :] = turn(inverse[:, b * width : (b + 1) * width])

    def step_back(e, came, gives):
        later = rows_of(e, 0, CHIPS).astype(jnp.float32)
        moved = []
        for j in range(2):
            ratio = weights[came] * inverse_norm[e, j]
            right = jnp.concatenate(
                [(ratio * later).astype(jnp.bfloat16), ratio.astype(jnp.bfloat16)], axis=1
            )
            both = nn_dot(kernel_rows[e, j], right)
            weights[gives, j * half : (j + 1) * half, :] = both[:, width:]
            moved.append(both[:, :width])
        return moved

    def gradient(e, moved, gives):
        part = jnp.zeros((width, width), jnp.float32)
        for j in range(2):
            span = slice(j * half, (j + 1) * half)
            residual = (moved[j] - predicted[e, span, :] * weights[gives, span, :]).astype(jnp.bfloat16)
            part = part + tn_dot(residual, columns_of(e, j * 4, j * 4 + 4))
        return part

    for slot in range(1, 4):
        arrive(slot)

        @pl.when(tm == 1)
        def _():
            middle(slot).start()

    spread_logs(0, 4)
    prepare(0, 0, 4)
    tile(0, 0, 0)

    @pl.when(tm == 0)
    def _():
        for slot in range(4):
            middle(slot).wait_recv()
        prepare(1, 0, 4)
        tile(1, 0, 0)

    @pl.when(tm == 1)
    def _():
        for slot in (4, 6):
            arrive(slot)
            for copy in sideways(slot):
                copy.start()
            middle(slot).start()
        for slot in (5, 7):
            arrive(slot)
            middle(slot).start()

    @pl.when(tm == 0)
    def _():
        for slot in range(4, CHIPS):
            arrive(slot)

    spread_logs(4, CHIPS)
    prepare(0, 4, CHIPS)
    tile(0, 1, 0)
    tall_tile(0)
    normalize(0)

    @pl.when(tm == 1)
    def _():
        last = jnp.exp(bias[1] - jnp.max(bias[1], axis=0, keepdims=True))
        weights[1] = last / jnp.sum(last, axis=0, keepdims=True)
        moved = step_back(0, 1, 0)
        for b in range(total // width):
            lean[b : b + 1, :] = weights[0, b * width : (b + 1) * width, :].T[0:1, :]
        lean_copy.start()
        score_mine[...] = gradient(0, moved, 0)

    @pl.when(tm == 0)
    def _():
        for slot in range(4, CHIPS):
            middle(slot).wait_recv()
        prepare(1, 4, CHIPS)
        tile(1, 1, 0)
        tall_tile(1)
        normalize(1)
        lean_copy.wait_recv()
        for b in range(total // width):
            weights[2, b * width : (b + 1) * width, :] = turn(lean[b : b + 1, :])
        moved = step_back(1, 2, 1)
        part = gradient(1, moved, 1)
        moved = step_back(0, 1, 0)
        score_mine[...] = part + gradient(0, moved, 0)

    score_copy.start()
    for k in range(2):
        smoothed_ref[k : k + 1, :] = weights[k, 0:rows, :].T[0:1, :] * total
    score_copy.wait_recv()
    score_ref[...] = (score_mine[...] + score_theirs[...]) * p_down

    for d in range(4):

        @pl.when(z != d)
        def _():
            for q in range(2):

                @pl.when(sends_to(d, q))
                def _():
                    for copy in own(slot_of(d, q), 2 * d + q):
                        copy.wait_send()

    for copy in own(1, across):
        copy.wait_send()
    score_copy.wait_send()

    @pl.when(tm == 1)
    def _():
        for slot in (4, 6):
            for copy in sideways(slot):
                copy.wait_send()
        for slot in range(CHIPS):
            middle(slot).wait_send()
        lean_copy.wait_send()


def hand_over(a_in, b_in, a_out, b_out, sems):
    leaving = [
        pltpu.make_async_copy(a_in, a_out, sems.at[0]),
        pltpu.make_async_copy(b_in, b_out, sems.at[1]),
    ]
    for copy in leaving:
        copy.start()
    for copy in leaving:
        copy.wait()


def fused(particles, log_weight, trans_weight, precision):
    steps_here, rows, width = particles.shape
    total = CHIPS * rows
    whole = pl.BlockSpec(memory_space=pltpu.VMEM)
    arguments = (
        particles.reshape(steps_here * rows, width), log_weight, trans_weight, precision.reshape(1, width)
    )
    smoothed, score = pl.pallas_call(
        smoother_kernel,
        out_shape=(
            pltpu.VMEM((steps_here, rows), jnp.float32),
            pltpu.VMEM((width, width), jnp.float32),
        ),
        in_specs=[pl.BlockSpec(memory_space=pltpu.HBM)] * 4,
        out_specs=(whole, whole),
        scratch_shapes=[
            pltpu.VMEM((CHIPS, steps_here, rows), jnp.float32),
            pltpu.VMEM((width, width), jnp.bfloat16),
            pltpu.VMEM((1, width), jnp.float32),
            pltpu.VMEM((CHIPS, 2 * rows, width), jnp.bfloat16),
            pltpu.VMEM((CHIPS, rows, width), jnp.bfloat16),
            pltpu.VMEM((2, 2, total // 2, total), jnp.bfloat16),
            pltpu.VMEM((2, 4, 8, total // 2), jnp.float32),
            pltpu.VMEM((2, 2, total, width), jnp.float32),
            pltpu.VMEM((2, total, width), jnp.float32),
            pltpu.VMEM((2, total, width), jnp.bfloat16),
            pltpu.VMEM((2, total, width), jnp.float32),
            pltpu.VMEM((3, total, width), jnp.float32),
            pltpu.VMEM((CHIPS, EXTRA, width), jnp.float32),
            pltpu.VMEM((8, width), jnp.float32),
            pltpu.VMEM((width, width), jnp.float32),
            pltpu.VMEM((width, width), jnp.float32),
            pltpu.SemaphoreType.DMA((4,)),
            pltpu.SemaphoreType.DMA((CHIPS,)),
            pltpu.SemaphoreType.DMA((CHIPS,)),
            pltpu.SemaphoreType.DMA((CHIPS + 2,)),
            pltpu.SemaphoreType.DMA((CHIPS,)),
            pltpu.SemaphoreType.DMA((CHIPS,)),
            pltpu.SemaphoreType.DMA((CHIPS,)),
            pltpu.SemaphoreType.DMA((2,)),
            pltpu.SemaphoreType.REGULAR((CHIPS,)),
        ],
        compiler_params=pltpu.CompilerParams(
            collective_id=0, has_side_effects=True, vmem_limit_bytes=40 * 2**20
        ),
    )(*[pltpu.with_memory_space_constraint(a, pltpu.HBM) for a in arguments])
    return pl.pallas_call(
        hand_over,
        out_shape=(
            jax.ShapeDtypeStruct((steps_here, rows), jnp.float32),
            jax.ShapeDtypeStruct((width, width), jnp.float32),
        ),
        in_specs=[whole] * 2,
        out_specs=(pl.BlockSpec(memory_space=pltpu.HBM),) * 2,
        scratch_shapes=[
            pltpu.SemaphoreType.DMA((2,)),
        ],
        compiler_params=pltpu.CompilerParams(vmem_limit_bytes=40 * 2**20),
    )(smoothed, score)


def plan(particles, log_weight, trans_weight, precision):
    steps_here, rows, width = particles.shape
    n_dom = lax.axis_size("dom")
    total = n_dom * rows
    small = total <= MOST_ROWS and total % (2 * width) == 0 and rows <= width and rows % 16 == 0
    shaped = n_dom == 8 and lax.axis_size("tm") == 2 and steps_here == 2 and width == 128
    if small and shaped:
        return fused(particles, log_weight, trans_weight, precision)
    return shards(particles, log_weight, trans_weight, precision)


def solution(mesh):
    placed = (P("tm", ("seq", "dom"), None), P("tm", ("seq", "dom")), P(), P())
    return jax.shard_map(
        plan,
        mesh=mesh,
        in_specs=placed,
        out_specs=(P("tm", ("seq", "dom")), P("seq", None)),
        check_vma=False,
    )
```

```python
import functools

import jax
import jax.numpy as jnp
from jax import lax
from jax.experimental import pallas as pl
from jax.experimental.pallas import tpu as pltpu
from jax.sharding import PartitionSpec as P

exact_mode = lax.Precision.HIGHEST


def from_behind(x, axis, by):
    size = lax.axis_size(axis)
    pairs = [(i, i + by) for i in range(size) if 0 <= i + by < size]
    return lax.ppermute(x, axis, pairs)


def block_size(length):
    best = 1
    for trial in range(1, min(length, 512) + 1):
        if length % trial == 0:
            best = trial
    return best


def project_rows(rows, precision, weight_full):
    return jnp.dot(rows.astype(jnp.float32) * precision, weight_full, precision=exact_mode).astype(
        jnp.bfloat16
    )


def pair_scores(row_proj, column_rows, column_bias):
    return (
        jnp.einsum("id,jd->ij", row_proj, column_rows, preferred_element_type=jnp.float32)
        + column_bias[None, :]
    )


def make_norm_fold(row_proj, bias_row, carried, block_in, first_row):
    length = block_in.shape[0]
    size = block_size(length)

    def inner(position, state):
        row_top, row_total = state
        offset = position * size
        column_rows = lax.dynamic_slice_in_dim(block_in, offset, size, 0)
        bias_part = lax.dynamic_slice_in_dim(bias_row, first_row + offset, size, 0)
        scores = pair_scores(row_proj, column_rows, bias_part)
        new_top = jnp.maximum(row_top, jnp.max(scores, axis=1))
        row_total = row_total * jnp.exp(row_top - new_top) + jnp.sum(
            jnp.exp(scores - new_top[:, None]), axis=1
        )
        return (new_top, row_total)

    return lax.fori_loop(0, length // size, inner, carried)


def make_column_fold(row_proj, bias_row, row_norm, row_weight, carried, block_in, first_row):
    length = block_in.shape[0]
    size = block_size(length)

    def inner(position, state):
        moved, column_sums = state
        offset = position * size
        column_rows = lax.dynamic_slice_in_dim(block_in, offset, size, 0)
        bias_part = lax.dynamic_slice_in_dim(bias_row, first_row + offset, size, 0)
        scores = pair_scores(row_proj, column_rows, bias_part)
        backward = (row_weight[:, None] * jnp.exp(scores - row_norm[:, None])).astype(jnp.bfloat16)
        moved = moved + jnp.dot(backward, column_rows, preferred_element_type=jnp.float32)
        column_sums = lax.dynamic_update_slice_in_dim(
            column_sums, jnp.sum(backward.astype(jnp.float32), axis=0), first_row + offset, 0
        )
        return (moved, column_sums)

    return lax.fori_loop(0, length // size, inner, carried)


def shards(particles, log_weight, trans_weight, precision):
    steps_here, rows_here, width = particles.shape
    tm_count = lax.axis_size("tm")
    dom_count = lax.axis_size("dom")
    total_rows = rows_here * dom_count
    tm_place = lax.axis_index("tm")
    is_last = tm_place == tm_count - 1
    weight_full = trans_weight.astype(jnp.float32)
    boundary = from_behind(particles[0], "tm", -1)
    later_sets = [particles[1]] + [boundary]
    later_proj = [project_rows(rows, precision, weight_full) for rows in later_sets]
    biases = []
    for k in range(steps_here):
        predicted = jnp.dot(particles[k], trans_weight.T, preferred_element_type=jnp.float32)
        biases.append(log_weight[k] - 0.5 * jnp.sum(precision * predicted * predicted, axis=1))
    local_bias = jnp.stack(biases)
    full_bias = lax.all_gather(local_bias, "dom", axis=1, tiled=True)
    row_norms = []
    whole = lax.all_gather(particles, "dom", axis=1, tiled=True)
    for k in range(steps_here):
        start_state = (
            jnp.full((rows_here,), -jnp.inf, jnp.float32),
            jnp.zeros((rows_here,), jnp.float32),
        )
        row_top, row_total = make_norm_fold(later_proj[k], full_bias[k], start_state, whole[k], 0)
        row_norms.append(row_top + jnp.log(row_total))
    final_logs = log_weight[steps_here - 1]
    global_top = lax.pmax(jnp.max(final_logs), "dom")
    global_total = lax.psum(jnp.sum(jnp.exp(final_logs - global_top)), "dom")
    final_weights = jnp.exp(final_logs - global_top) / global_total
    carried = (
        jnp.zeros((steps_here, rows_here), jnp.float32),
        jnp.zeros((width, width), jnp.float32),
    )
    for r in range(tm_count):
        if r == 0:
            incoming = jnp.zeros((rows_here,), jnp.float32)
        else:
            incoming = from_behind(carried[0][0], "tm", -1)
        owner = tm_count - 1 - r
        backward_partial_value = jnp.zeros((width, width), jnp.float32)
        outputs = [None] * steps_here
        row_weight = incoming
        for backward_k in range(steps_here - 1, -1, -1):
            column_rows = particles[backward_k]
            backward_start_state = (
                jnp.zeros((rows_here, width), jnp.float32),
                jnp.zeros((total_rows,), jnp.float32),
            )
            moved, column_sums = make_column_fold(
                later_proj[backward_k],
                full_bias[backward_k],
                row_norms[backward_k],
                row_weight,
                backward_start_state,
                whole[backward_k],
                0,
            )
            column_weights = lax.psum_scatter(column_sums, "dom", scatter_dimension=0, tiled=True)
            outer = jnp.dot(
                later_sets[backward_k].astype(jnp.float32).T, moved, precision=exact_mode
            )
            column_float = column_rows.astype(jnp.float32)
            moment = jnp.dot(
                column_float.T * column_weights[None, :], column_float, precision=exact_mode
            )
            backward_partial_value = backward_partial_value + precision[:, None] * (
                outer - jnp.dot(weight_full, moment, precision=exact_mode)
            )
            if backward_k == steps_here - 1:
                column_weights = jnp.where(is_last, final_weights, column_weights)
            outputs[backward_k] = column_weights
            row_weight = column_weights
        is_owner = tm_place == owner
        carried = (
            jnp.where(is_owner, jnp.stack(outputs), carried[0]),
            jnp.where(is_owner, backward_partial_value, carried[1]),
        )
    stacked, partial_value = carried
    score = lax.psum(partial_value, ("dom", "tm"))
    return (stacked * total_rows, score)


MESH = pl.DeviceIdType.MESH
EXTRA = 16
CHIPS = 8
EARLY = 6
LANES_ONE = 6
MOST_ROWS = 1024


def nt_dot(a, b):
    return lax.dot_general(a, b, (((1,), (1,)), ((), ())), preferred_element_type=jnp.float32)


def tn_dot(a, b):
    return lax.dot_general(a, b, (((0,), (0,)), ((), ())), preferred_element_type=jnp.float32)


def nn_dot(a, b):
    return jnp.dot(a, b, preferred_element_type=jnp.float32)


def split_three(x):
    high = x.astype(jnp.bfloat16)
    rest = x - high.astype(jnp.float32)
    middle = rest.astype(jnp.bfloat16)
    low = (rest - middle.astype(jnp.float32)).astype(jnp.bfloat16)
    return high, middle, low


def smoother_kernel(
    x_hbm, lw_hbm, w_hbm, p_hbm, smoothed_ref, score_ref,
    lw_held, w_ref, p_ref, held, middle_rows, kernel_rows, stats, inverse_norm, bias, projected, predicted,
    weights, stage, lean, score_mine, score_theirs,
    in_sem, send_sem, lw_send_sem, inside_send_sem, recv_sem, lw_sem, inside_sem, late_sem, up_sem,
):
    width = x_hbm.shape[1]
    rows = x_hbm.shape[0] // 2
    total = CHIPS * rows
    dom = lax.axis_index("dom")
    tm = lax.axis_index("tm")
    z, side = dom // 2, dom % 2
    across = dom + 1 - 2 * side
    other = 1 - tm

    def slot_of(d, q):
        high, low, turned = [
            here + there - 2 * here * there for here, there in ((z // 2, d // 2), (z % 2, d % 2), (side, q))
        ]
        return 4 * high + 2 * low + turned + tm * high * (turned - low)

    loads = [
        pltpu.make_async_copy(source, target, in_sem.at[i])
        for i, (source, target) in enumerate(
            [(lw_hbm, lw_held.at[0]), (w_hbm, w_ref), (p_hbm, p_ref), (x_hbm, held.at[0])]
        )
    ]
    barrier = pltpu.get_barrier_semaphore()

    def signal(sem, to_dom, to_tm):
        pl.semaphore_signal(sem, inc=1, device_id={"dom": to_dom, "tm": to_tm}, device_id_type=MESH)

    for d in range(1, 4):

        @pl.when(z < d)
        def _():
            for q in range(2):
                signal(barrier, 2 * d + q, tm)

    signal(barrier, across, tm)
    signal(barrier, dom, other)

    def remote(source, target, send, recv, to_dom, to_tm):
        return pltpu.make_async_remote_copy(
            src_ref=source,
            dst_ref=target,
            send_sem=send,
            recv_sem=recv,
            device_id={"dom": to_dom, "tm": to_tm},
            device_id_type=MESH,
        )

    def own(slot, to_dom):
        return (
            remote(lw_hbm, lw_held.at[slot], lw_send_sem.at[slot], lw_sem.at[slot], to_dom, tm),
            remote(x_hbm, held.at[slot], send_sem.at[slot], recv_sem.at[slot], to_dom, tm),
        )

    def start_own(d, q):
        def start():
            for copy in own(slot_of(d, q), 2 * d + q):
                copy.start()

        pl.when(sends_to(d, q))(start)

    def sends_to(d, q):
        same_half = z // 2 == d // 2
        return jnp.logical_or(jnp.logical_or(same_half, tm == 0), side == q)

    def sideways(slot):
        return (
            remote(
                lw_held.at[slot], lw_held.at[slot + 2], lw_send_sem.at[slot + 2], lw_sem.at[slot + 2], across, tm
            ),
            remote(held.at[slot], held.at[slot + 2], send_sem.at[slot + 2], recv_sem.at[slot + 2], across, tm),
        )

    def middle(slot):
        source = x_hbm if slot == 0 else held.at[slot]
        return remote(
            source.at[0:rows], middle_rows.at[slot], inside_send_sem.at[slot], inside_sem.at[slot], dom, other
        )

    lean_copy = remote(lean, lean, inside_send_sem.at[CHIPS], late_sem.at[0], dom, other)
    score_copy = remote(score_mine, score_theirs, inside_send_sem.at[CHIPS + 1], late_sem.at[1], dom, other)

    pl.semaphore_wait(barrier, 2 + 2 * z)
    for d in range(3):

        @pl.when(z > d)
        def _():
            for q in range(2):
                signal(up_sem.at[slot_of(d, q)], 2 * d + q, tm)

    for d, turn_of in ((0, tm >= 0), (1, tm == 1), (2, tm >= 0), (1, tm == 0)):

        @pl.when(jnp.logical_and(z > d, turn_of))
        def _():
            for q in range(2):
                start_own(d, q)

    for copy in own(1, across):
        copy.start()

    @pl.when(tm == 1)
    def _():
        middle(0).start()

    for load in loads:
        load.start()

    for d in range(1, 4):

        @pl.when(z < d)
        def _():
            for q in range(2):
                pl.semaphore_wait(up_sem.at[slot_of(d, q)], 1)
                start_own(d, q)

    stage[...] = jnp.zeros_like(stage)
    for load in loads:
        load.wait()

    def arrive(slot):
        for copy in own(slot, across):
            copy.wait_recv()

    weight = w_ref[...]
    p_row = p_ref[...]
    p_down = jnp.broadcast_to(p_row, (width, width)).T
    scaled = jnp.concatenate(split_three(p_down * weight.astype(jnp.float32)), axis=1)
    line = lax.broadcasted_iota(jnp.int32, (EXTRA, 2 * width), 0)
    which = lax.broadcasted_iota(jnp.int32, (EXTRA, 2 * width), 1) // width
    pick = jnp.where((line < 6) & (line % 2 == which), 1.0, 0.0).astype(jnp.bfloat16)

    def flat(block):
        return block.reshape(block.shape[0] * rows, width)

    def columns_of(e, first, last):
        return flat(held[first:last, e * rows : (e + 1) * rows, :])

    def rows_of(e, first, last):
        return flat(middle_rows[first:last] if e else held[first:last, rows:, :])

    def spread_logs(first, last):
        for r in range(first, last):
            for n, value in enumerate(split_three(lw_held[r])):
                stage[r, 2 * n : 2 * n + 2, 0:rows] = value.astype(jnp.float32)
            spread = tn_dot(stage[r].astype(jnp.bfloat16), pick)
            for e in range(2):
                bias[e, r * rows : (r + 1) * rows, :] = spread[:rows, e * width : (e + 1) * width]

    def prepare_columns(e, first, last):
        span = slice(first * rows, last * rows)
        mean = nt_dot(columns_of(e, first, last), weight)
        predicted[e, span, :] = mean
        energy = jnp.sum(p_row * mean * mean, axis=1, keepdims=True)
        bias[e, span, :] = bias[e, span, :] - 0.5 * energy

    def prepare_rows(e, first, last):
        wide = nn_dot(rows_of(e, first, last), scaled)
        projected[e, first * rows : last * rows, :] = (
            wide[:, :width] + (wide[:, width : 2 * width] + wide[:, 2 * width :])
        ).astype(jnp.bfloat16)

    class Cut:
        def __init__(self, e, columns, lanes):
            self.e, self.first = e, lanes * rows // width * width
            self.ranks = ((0, columns), (columns, CHIPS))
            self.spans = [slice(a * rows, b * rows) for a, b in self.ranks]

    def exponentials(e, first, last, lanes):
        span = slice(first * rows, last * rows)
        scores = nt_dot(columns_of(e, first, last), projected[e, lanes, :])
        scores = scores + jnp.concatenate([bias[e, span, :]] * ((lanes.stop - lanes.start) // width), axis=1)
        top = jnp.max(scores, axis=0, keepdims=True)
        terms = jnp.exp(scores - top)
        kernel_rows[e, span, lanes] = terms.astype(jnp.bfloat16)
        return top, jnp.sum(terms, axis=0, keepdims=True)

    def tile(cut, c):
        e, lanes = cut.e, slice(0, cut.first)
        top, norm = exponentials(e, *cut.ranks[c], lanes)
        stats[e, c, 0:1, lanes] = top
        stats[e, c, 1:2, lanes] = norm

    def tall_tile(cut):
        e, lanes = cut.e, slice(cut.first, total)
        top, norm = exponentials(e, 0, CHIPS, lanes)
        stats[e, 0, 0:1, lanes] = top
        stats[e, 0, 1:2, lanes] = norm

    def turn(row):
        return jnp.broadcast_to(row, (width, width)).T

    def blocks(lanes):
        return [slice(at, at + width) for at in range(lanes.start, lanes.stop, width)]

    def normalize(cut):
        e, lanes = cut.e, slice(0, cut.first)
        tops = [stats[e, c, 0:1, lanes] for c in range(2)]
        top = jnp.maximum(tops[0], tops[1])
        scales = [jnp.exp(tops[c] - top) for c in range(2)]
        norm = sum(scales[c] * stats[e, c, 1:2, lanes] for c in range(2))
        for c in range(2):
            inverse = scales[c] / norm
            for block in blocks(lanes):
                inverse_norm[e, c, block, :] = turn(inverse[:, block])
        lanes = slice(cut.first, total)
        inverse = 1.0 / stats[e, 0, 1:2, lanes]
        for block, source in zip(blocks(lanes), blocks(slice(0, total - cut.first))):
            inverse_norm[e, 0, block, :] = turn(inverse[:, source])

    def ratios(cut, came):
        e, lanes, rest = cut.e, slice(0, cut.first), slice(cut.first, total)
        below = weights[came, rest, :] * inverse_norm[e, 0, rest, :]
        return [
            jnp.concatenate([weights[came, lanes, :] * inverse_norm[e, c, lanes, :], below], axis=0)
            for c in range(2)
        ]

    def weigh(cut, came, gives):
        e, spans, ranks = cut.e, cut.spans, cut.ranks
        for c, ratio in enumerate(ratios(cut, came)):
            weights[gives, spans[c], :] = nn_dot(kernel_rows[e, spans[c], :], ratio.astype(jnp.bfloat16))

    def move(cut, came):
        e, spans, ranks = cut.e, cut.spans, cut.ranks
        later = rows_of(e, 0, CHIPS).astype(jnp.float32)
        return [
            nn_dot(kernel_rows[e, spans[c], :], (ratio * later).astype(jnp.bfloat16))
            for c, ratio in enumerate(ratios(cut, came))
        ]

    def step_back(cut, came, gives):
        e, spans, ranks = cut.e, cut.spans, cut.ranks
        later = rows_of(e, 0, CHIPS).astype(jnp.float32)
        moved = []
        for c, ratio in enumerate(ratios(cut, came)):
            right = jnp.concatenate(
                [(ratio * later).astype(jnp.bfloat16), ratio.astype(jnp.bfloat16)], axis=1
            )
            both = nn_dot(kernel_rows[e, spans[c], :], right)
            weights[gives, spans[c], :] = both[:, width:]
            moved.append(both[:, :width])
        return moved

    def gradient(cut, moved, gives):
        e, spans, ranks = cut.e, cut.spans, cut.ranks
        part = jnp.zeros((width, width), jnp.float32)
        for c in range(2):
            residual = moved[c] - predicted[e, spans[c], :] * weights[gives, spans[c], :]
            part = part + tn_dot(residual.astype(jnp.bfloat16), columns_of(e, *ranks[c]))
        return part

    for slot in range(1, 4):
        arrive(slot)

        @pl.when(tm == 1)
        def _():
            middle(slot).start()

    @pl.when(tm == 1)
    def _():
        cut = Cut(0, EARLY, EARLY)
        for slot in range(4, EARLY):
            arrive(slot)
            for copy in sideways(slot):
                copy.start()
            middle(slot).start()
        spread_logs(0, EARLY)
        prepare_columns(0, 0, EARLY)
        prepare_rows(0, 0, EARLY)
        tile(cut, 0)
        for slot in range(EARLY, CHIPS):
            arrive(slot)
            middle(slot).start()
        spread_logs(EARLY, CHIPS)
        prepare_columns(0, EARLY, CHIPS)
        prepare_rows(0, EARLY, CHIPS)
        tile(cut, 1)
        tall_tile(cut)
        normalize(cut)
        last = jnp.exp(bias[1] - jnp.max(bias[1], axis=0, keepdims=True))
        weights[1] = last / jnp.sum(last, axis=0, keepdims=True)
        weigh(cut, 1, 0)
        for b, block in enumerate(blocks(slice(0, total))):
            lean[b : b + 1, :] = weights[0, block, :].T[0:1, :]
        lean_copy.start()
        score_mine[...] = gradient(cut, move(cut, 1), 0)

    @pl.when(tm == 0)
    def _():
        zero, one = Cut(0, 4, 4), Cut(1, 4, LANES_ONE)
        spread_logs(0, 4)
        for e in range(2):
            prepare_columns(e, 0, 4)
        prepare_rows(0, 0, 4)
        tile(zero, 0)
        for slot in range(LANES_ONE):
            middle(slot).wait_recv()
        prepare_rows(1, 0, LANES_ONE)
        tile(one, 0)
        for slot in range(4, CHIPS):
            arrive(slot)
        spread_logs(4, CHIPS)
        for e in range(2):
            prepare_columns(e, 4, CHIPS)
        prepare_rows(0, 4, CHIPS)
        tile(zero, 1)
        tall_tile(zero)
        normalize(zero)
        tile(one, 1)
        for slot in range(LANES_ONE, CHIPS):
            middle(slot).wait_recv()
        prepare_rows(1, LANES_ONE, CHIPS)
        tall_tile(one)
        normalize(one)
        lean_copy.wait_recv()
        for b, block in enumerate(blocks(slice(0, total))):
            weights[2, block, :] = turn(lean[b : b + 1, :])
        moved = step_back(one, 2, 1)
        part = gradient(one, moved, 1)
        moved = step_back(zero, 1, 0)
        score_mine[...] = part + gradient(zero, moved, 0)

    score_copy.start()
    for k in range(2):
        smoothed_ref[k : k + 1, :] = weights[k, 0:rows, :].T[0:1, :] * total
    score_copy.wait_recv()
    score_ref[...] = (score_mine[...] + score_theirs[...]) * p_down

    for d in range(4):

        @pl.when(z != d)
        def _():
            for q in range(2):

                @pl.when(sends_to(d, q))
                def _():
                    for copy in own(slot_of(d, q), 2 * d + q):
                        copy.wait_send()

    for copy in own(1, across):
        copy.wait_send()
    score_copy.wait_send()

    @pl.when(tm == 1)
    def _():
        for slot in range(4, EARLY):
            for copy in sideways(slot):
                copy.wait_send()
        for slot in range(CHIPS):
            middle(slot).wait_send()
        lean_copy.wait_send()


def hand_over(a_in, b_in, a_out, b_out, sems):
    leaving = [
        pltpu.make_async_copy(a_in, a_out, sems.at[0]),
        pltpu.make_async_copy(b_in, b_out, sems.at[1]),
    ]
    for copy in leaving:
        copy.start()
    for copy in leaving:
        copy.wait()


def fused(particles, log_weight, trans_weight, precision):
    steps_here, rows, width = particles.shape
    total = CHIPS * rows
    whole = pl.BlockSpec(memory_space=pltpu.VMEM)
    arguments = (
        particles.reshape(steps_here * rows, width), log_weight, trans_weight, precision.reshape(1, width)
    )
    smoothed, score = pl.pallas_call(
        smoother_kernel,
        out_shape=(
            pltpu.VMEM((steps_here, rows), jnp.float32),
            pltpu.VMEM((width, width), jnp.float32),
        ),
        in_specs=[pl.BlockSpec(memory_space=pltpu.HBM)] * 4,
        out_specs=(whole, whole),
        scratch_shapes=[
            pltpu.VMEM((CHIPS, steps_here, rows), jnp.float32),
            pltpu.VMEM((width, width), jnp.bfloat16),
            pltpu.VMEM((1, width), jnp.float32),
            pltpu.VMEM((CHIPS, 2 * rows, width), jnp.bfloat16),
            pltpu.VMEM((CHIPS, rows, width), jnp.bfloat16),
            pltpu.VMEM((2, total, total), jnp.bfloat16),
            pltpu.VMEM((2, 2, 8, total), jnp.float32),
            pltpu.VMEM((2, 2, total, width), jnp.float32),
            pltpu.VMEM((2, total, width), jnp.float32),
            pltpu.VMEM((2, total, width), jnp.bfloat16),
            pltpu.VMEM((2, total, width), jnp.float32),
            pltpu.VMEM((3, total, width), jnp.float32),
            pltpu.VMEM((CHIPS, EXTRA, width), jnp.float32),
            pltpu.VMEM((8, width), jnp.float32),
            pltpu.VMEM((width, width), jnp.float32),
            pltpu.VMEM((width, width), jnp.float32),
            pltpu.SemaphoreType.DMA((4,)),
            pltpu.SemaphoreType.DMA((CHIPS,)),
            pltpu.SemaphoreType.DMA((CHIPS,)),
            pltpu.SemaphoreType.DMA((CHIPS + 2,)),
            pltpu.SemaphoreType.DMA((CHIPS,)),
            pltpu.SemaphoreType.DMA((CHIPS,)),
            pltpu.SemaphoreType.DMA((CHIPS,)),
            pltpu.SemaphoreType.DMA((2,)),
            pltpu.SemaphoreType.REGULAR((CHIPS,)),
        ],
        compiler_params=pltpu.CompilerParams(
            collective_id=0, has_side_effects=True, vmem_limit_bytes=40 * 2**20
        ),
    )(*[pltpu.with_memory_space_constraint(a, pltpu.HBM) for a in arguments])
    return pl.pallas_call(
        hand_over,
        out_shape=(
            jax.ShapeDtypeStruct((steps_here, rows), jnp.float32),
            jax.ShapeDtypeStruct((width, width), jnp.float32),
        ),
        in_specs=[whole] * 2,
        out_specs=(pl.BlockSpec(memory_space=pltpu.HBM),) * 2,
        scratch_shapes=[
            pltpu.SemaphoreType.DMA((2,)),
        ],
        compiler_params=pltpu.CompilerParams(vmem_limit_bytes=40 * 2**20),
    )(smoothed, score)


def plan(particles, log_weight, trans_weight, precision):
    steps_here, rows, width = particles.shape
    n_dom = lax.axis_size("dom")
    total = n_dom * rows
    small = total <= MOST_ROWS and total % (2 * width) == 0 and rows <= width and rows % 16 == 0
    shaped = n_dom == 8 and lax.axis_size("tm") == 2 and steps_here == 2 and width == 128
    if small and shaped:
        return fused(particles, log_weight, trans_weight, precision)
    return shards(particles, log_weight, trans_weight, precision)


def solution(mesh):
    placed = (P("tm", ("seq", "dom"), None), P("tm", ("seq", "dom")), P(), P())
    return jax.shard_map(
        plan,
        mesh=mesh,
        in_specs=placed,
        out_specs=(P("tm", ("seq", "dom")), P("seq", None)),
        check_vma=False,
    )
```

```python
import functools

import jax
import jax.numpy as jnp
from jax import lax
from jax.experimental import pallas as pl
from jax.experimental.pallas import tpu as pltpu
from jax.sharding import PartitionSpec as P

exact_mode = lax.Precision.HIGHEST


def from_behind(x, axis, by):
    size = lax.axis_size(axis)
    pairs = [(i, i + by) for i in range(size) if 0 <= i + by < size]
    return lax.ppermute(x, axis, pairs)


def block_size(length):
    best = 1
    for trial in range(1, min(length, 512) + 1):
        if length % trial == 0:
            best = trial
    return best


def project_rows(rows, precision, weight_full):
    return jnp.dot(rows.astype(jnp.float32) * precision, weight_full, precision=exact_mode).astype(
        jnp.bfloat16
    )


def pair_scores(row_proj, column_rows, column_bias):
    return (
        jnp.einsum("id,jd->ij", row_proj, column_rows, preferred_element_type=jnp.float32)
        + column_bias[None, :]
    )


def make_norm_fold(row_proj, bias_row, carried, block_in, first_row):
    length = block_in.shape[0]
    size = block_size(length)

    def inner(position, state):
        row_top, row_total = state
        offset = position * size
        column_rows = lax.dynamic_slice_in_dim(block_in, offset, size, 0)
        bias_part = lax.dynamic_slice_in_dim(bias_row, first_row + offset, size, 0)
        scores = pair_scores(row_proj, column_rows, bias_part)
        new_top = jnp.maximum(row_top, jnp.max(scores, axis=1))
        row_total = row_total * jnp.exp(row_top - new_top) + jnp.sum(
            jnp.exp(scores - new_top[:, None]), axis=1
        )
        return (new_top, row_total)

    return lax.fori_loop(0, length // size, inner, carried)


def make_column_fold(row_proj, bias_row, row_norm, row_weight, carried, block_in, first_row):
    length = block_in.shape[0]
    size = block_size(length)

    def inner(position, state):
        moved, column_sums = state
        offset = position * size
        column_rows = lax.dynamic_slice_in_dim(block_in, offset, size, 0)
        bias_part = lax.dynamic_slice_in_dim(bias_row, first_row + offset, size, 0)
        scores = pair_scores(row_proj, column_rows, bias_part)
        backward = (row_weight[:, None] * jnp.exp(scores - row_norm[:, None])).astype(jnp.bfloat16)
        moved = moved + jnp.dot(backward, column_rows, preferred_element_type=jnp.float32)
        column_sums = lax.dynamic_update_slice_in_dim(
            column_sums, jnp.sum(backward.astype(jnp.float32), axis=0), first_row + offset, 0
        )
        return (moved, column_sums)

    return lax.fori_loop(0, length // size, inner, carried)


def shards(particles, log_weight, trans_weight, precision):
    steps_here, rows_here, width = particles.shape
    tm_count = lax.axis_size("tm")
    dom_count = lax.axis_size("dom")
    total_rows = rows_here * dom_count
    tm_place = lax.axis_index("tm")
    is_last = tm_place == tm_count - 1
    weight_full = trans_weight.astype(jnp.float32)
    boundary = from_behind(particles[0], "tm", -1)
    later_sets = [particles[1]] + [boundary]
    later_proj = [project_rows(rows, precision, weight_full) for rows in later_sets]
    biases = []
    for k in range(steps_here):
        predicted = jnp.dot(particles[k], trans_weight.T, preferred_element_type=jnp.float32)
        biases.append(log_weight[k] - 0.5 * jnp.sum(precision * predicted * predicted, axis=1))
    local_bias = jnp.stack(biases)
    full_bias = lax.all_gather(local_bias, "dom", axis=1, tiled=True)
    row_norms = []
    whole = lax.all_gather(particles, "dom", axis=1, tiled=True)
    for k in range(steps_here):
        start_state = (
            jnp.full((rows_here,), -jnp.inf, jnp.float32),
            jnp.zeros((rows_here,), jnp.float32),
        )
        row_top, row_total = make_norm_fold(later_proj[k], full_bias[k], start_state, whole[k], 0)
        row_norms.append(row_top + jnp.log(row_total))
    final_logs = log_weight[steps_here - 1]
    global_top = lax.pmax(jnp.max(final_logs), "dom")
    global_total = lax.psum(jnp.sum(jnp.exp(final_logs - global_top)), "dom")
    final_weights = jnp.exp(final_logs - global_top) / global_total
    carried = (
        jnp.zeros((steps_here, rows_here), jnp.float32),
        jnp.zeros((width, width), jnp.float32),
    )
    for r in range(tm_count):
        if r == 0:
            incoming = jnp.zeros((rows_here,), jnp.float32)
        else:
            incoming = from_behind(carried[0][0], "tm", -1)
        owner = tm_count - 1 - r
        backward_partial_value = jnp.zeros((width, width), jnp.float32)
        outputs = [None] * steps_here
        row_weight = incoming
        for backward_k in range(steps_here - 1, -1, -1):
            column_rows = particles[backward_k]
            backward_start_state = (
                jnp.zeros((rows_here, width), jnp.float32),
                jnp.zeros((total_rows,), jnp.float32),
            )
            moved, column_sums = make_column_fold(
                later_proj[backward_k],
                full_bias[backward_k],
                row_norms[backward_k],
                row_weight,
                backward_start_state,
                whole[backward_k],
                0,
            )
            column_weights = lax.psum_scatter(column_sums, "dom", scatter_dimension=0, tiled=True)
            outer = jnp.dot(
                later_sets[backward_k].astype(jnp.float32).T, moved, precision=exact_mode
            )
            column_float = column_rows.astype(jnp.float32)
            moment = jnp.dot(
                column_float.T * column_weights[None, :], column_float, precision=exact_mode
            )
            backward_partial_value = backward_partial_value + precision[:, None] * (
                outer - jnp.dot(weight_full, moment, precision=exact_mode)
            )
            if backward_k == steps_here - 1:
                column_weights = jnp.where(is_last, final_weights, column_weights)
            outputs[backward_k] = column_weights
            row_weight = column_weights
        is_owner = tm_place == owner
        carried = (
            jnp.where(is_owner, jnp.stack(outputs), carried[0]),
            jnp.where(is_owner, backward_partial_value, carried[1]),
        )
    stacked, partial_value = carried
    score = lax.psum(partial_value, ("dom", "tm"))
    return (stacked * total_rows, score)


MESH = pl.DeviceIdType.MESH
EXTRA = 16
CHIPS = 8
EARLY = 6
LANES_ONE = 6
MOST_ROWS = 1024


def nt_dot(a, b):
    return lax.dot_general(a, b, (((1,), (1,)), ((), ())), preferred_element_type=jnp.float32)


def tn_dot(a, b):
    return lax.dot_general(a, b, (((0,), (0,)), ((), ())), preferred_element_type=jnp.float32)


def nn_dot(a, b):
    return jnp.dot(a, b, preferred_element_type=jnp.float32)


def split_three(x):
    high = x.astype(jnp.bfloat16)
    rest = x - high.astype(jnp.float32)
    middle = rest.astype(jnp.bfloat16)
    low = (rest - middle.astype(jnp.float32)).astype(jnp.bfloat16)
    return high, middle, low


def smoother_kernel(
    x_hbm, lw_hbm, w_hbm, p_hbm, smoothed_ref, score_ref,
    lw_held, w_ref, p_ref, held, middle_rows, kernel_rows, stats, inverse_norm, bias, projected, predicted,
    weights, stage, lean, score_mine, score_theirs,
    in_sem, send_sem, lw_send_sem, inside_send_sem, recv_sem, lw_sem, inside_sem, late_sem, up_sem,
):
    width = x_hbm.shape[1]
    rows = x_hbm.shape[0] // 2
    total = CHIPS * rows
    dom = lax.axis_index("dom")
    tm = lax.axis_index("tm")
    z, side = dom // 2, dom % 2
    across = dom + 1 - 2 * side
    other = 1 - tm

    def slot_of(d, q):
        high, low, turned = [
            here + there - 2 * here * there for here, there in ((z // 2, d // 2), (z % 2, d % 2), (side, q))
        ]
        return 4 * high + 2 * low + turned + tm * high * (turned - low)

    loads = [
        pltpu.make_async_copy(source, target, in_sem.at[i])
        for i, (source, target) in enumerate(
            [(lw_hbm, lw_held.at[0]), (w_hbm, w_ref), (p_hbm, p_ref), (x_hbm, held.at[0])]
        )
    ]
    barrier = pltpu.get_barrier_semaphore()

    def signal(sem, to_dom, to_tm):
        pl.semaphore_signal(sem, inc=1, device_id={"dom": to_dom, "tm": to_tm}, device_id_type=MESH)

    for d in range(1, 4):

        @pl.when(z < d)
        def _():
            for q in range(2):
                signal(barrier, 2 * d + q, tm)

    signal(barrier, across, tm)
    signal(barrier, dom, other)

    def remote(source, target, send, recv, to_dom, to_tm):
        return pltpu.make_async_remote_copy(
            src_ref=source,
            dst_ref=target,
            send_sem=send,
            recv_sem=recv,
            device_id={"dom": to_dom, "tm": to_tm},
            device_id_type=MESH,
        )

    def own(slot, to_dom):
        return (
            remote(lw_hbm, lw_held.at[slot], lw_send_sem.at[slot], lw_sem.at[slot], to_dom, tm),
            remote(x_hbm, held.at[slot], send_sem.at[slot], recv_sem.at[slot], to_dom, tm),
        )

    def start_own(d, q):
        def start():
            for copy in own(slot_of(d, q), 2 * d + q):
                copy.start()

        pl.when(sends_to(d, q))(start)

    def sends_to(d, q):
        crossed = side == q
        if d == 3:
            crossed = jnp.logical_and(crossed, z != 1)
        return jnp.logical_or(jnp.logical_or(z // 2 == d // 2, tm == 0), crossed)

    near = 2 * (z + 1 - 2 * (z % 2)) + side
    corner = 2 * (z + 1 - 2 * (z % 2)) + 1 - side

    def pass_on(source, slot, to_dom):
        index = CHIPS + 4 * (source - 4) + slot - 4
        return (
            remote(lw_held.at[source], lw_held.at[slot], lw_send_sem.at[index], lw_sem.at[slot], to_dom, tm),
            remote(held.at[source], held.at[slot], send_sem.at[index], recv_sem.at[slot], to_dom, tm),
        )

    def passes(do, ready):
        def run(source, *ways):
            ready(source)
            for slot, to_dom in ways:
                for copy in pass_on(source, slot, to_dom):
                    do(copy)

        @pl.when(z < 2)
        def _():
            run(4, (6, across))
            run(5, (7, across))

        @pl.when(z == 2)
        def _():
            run(5, (4, near), (6, corner), (7, across))
            run(4, (6, across))

        @pl.when(z == 3)
        def _():
            run(5, (7, across))
            ready(4)

    def middle(slot):
        source = x_hbm if slot == 0 else held.at[slot]
        return remote(
            source.at[0:rows], middle_rows.at[slot], inside_send_sem.at[slot], inside_sem.at[slot], dom, other
        )

    lean_copy = remote(lean, lean, inside_send_sem.at[CHIPS], late_sem.at[0], dom, other)
    score_copy = remote(score_mine, score_theirs, inside_send_sem.at[CHIPS + 1], late_sem.at[1], dom, other)

    pl.semaphore_wait(barrier, 2 + 2 * z)
    for d in range(3):

        @pl.when(z > d)
        def _():
            for q in range(2):
                signal(up_sem.at[slot_of(d, q)], 2 * d + q, tm)

    for d, turn_of in ((0, tm >= 0), (1, tm == 1), (2, tm >= 0), (1, tm == 0)):

        @pl.when(jnp.logical_and(z > d, turn_of))
        def _():
            for q in range(2):
                start_own(d, q)

    for copy in own(1, across):
        copy.start()

    @pl.when(tm == 1)
    def _():
        middle(0).start()

    for load in loads:
        load.start()

    for d in range(1, 4):

        @pl.when(z < d)
        def _():
            for q in range(2):
                pl.semaphore_wait(up_sem.at[slot_of(d, q)], 1)
                start_own(d, q)

    stage[...] = jnp.zeros_like(stage)
    for load in loads:
        load.wait()

    def arrive(slot):
        for copy in own(slot, across):
            copy.wait_recv()

    weight = w_ref[...]
    p_row = p_ref[...]
    p_down = jnp.broadcast_to(p_row, (width, width)).T
    scaled = jnp.concatenate(split_three(p_down * weight.astype(jnp.float32)), axis=1)
    line = lax.broadcasted_iota(jnp.int32, (EXTRA, 2 * width), 0)
    which = lax.broadcasted_iota(jnp.int32, (EXTRA, 2 * width), 1) // width
    pick = jnp.where((line < 6) & (line % 2 == which), 1.0, 0.0).astype(jnp.bfloat16)

    def flat(block):
        return block.reshape(block.shape[0] * rows, width)

    def columns_of(e, first, last):
        return flat(held[first:last, e * rows : (e + 1) * rows, :])

    def rows_of(e, first, last):
        return flat(middle_rows[first:last] if e else held[first:last, rows:, :])

    def spread_logs(first, last):
        for r in range(first, last):
            for n, value in enumerate(split_three(lw_held[r])):
                stage[r, 2 * n : 2 * n + 2, 0:rows] = value.astype(jnp.float32)
            spread = tn_dot(stage[r].astype(jnp.bfloat16), pick)
            for e in range(2):
                bias[e, r * rows : (r + 1) * rows, :] = spread[:rows, e * width : (e + 1) * width]

    def prepare_columns(e, first, last):
        span = slice(first * rows, last * rows)
        mean = nt_dot(columns_of(e, first, last), weight)
        predicted[e, span, :] = mean
        energy = jnp.sum(p_row * mean * mean, axis=1, keepdims=True)
        bias[e, span, :] = bias[e, span, :] - 0.5 * energy

    def prepare_rows(e, first, last):
        wide = nn_dot(rows_of(e, first, last), scaled)
        projected[e, first * rows : last * rows, :] = (
            wide[:, :width] + (wide[:, width : 2 * width] + wide[:, 2 * width :])
        ).astype(jnp.bfloat16)

    class Cut:
        def __init__(self, e, columns, lanes):
            self.e, self.first = e, lanes * rows // width * width
            self.ranks = ((0, columns), (columns, CHIPS))
            self.spans = [slice(a * rows, b * rows) for a, b in self.ranks]

    def exponentials(e, first, last, lanes):
        span = slice(first * rows, last * rows)
        scores = nt_dot(columns_of(e, first, last), projected[e, lanes, :])
        scores = scores + jnp.concatenate([bias[e, span, :]] * ((lanes.stop - lanes.start) // width), axis=1)
        top = jnp.max(scores, axis=0, keepdims=True)
        terms = jnp.exp(scores - top)
        kernel_rows[e, span, lanes] = terms.astype(jnp.bfloat16)
        return top, jnp.sum(terms, axis=0, keepdims=True)

    def tile(cut, c):
        e, lanes = cut.e, slice(0, cut.first)
        top, norm = exponentials(e, *cut.ranks[c], lanes)
        stats[e, c, 0:1, lanes] = top
        stats[e, c, 1:2, lanes] = norm

    def tall_tile(cut):
        e, lanes = cut.e, slice(cut.first, total)
        top, norm = exponentials(e, 0, CHIPS, lanes)
        stats[e, 0, 0:1, lanes] = top
        stats[e, 0, 1:2, lanes] = norm

    def turn(row):
        return jnp.broadcast_to(row, (width, width)).T

    def blocks(lanes):
        return [slice(at, at + width) for at in range(lanes.start, lanes.stop, width)]

    def normalize(cut):
        e, lanes = cut.e, slice(0, cut.first)
        tops = [stats[e, c, 0:1, lanes] for c in range(2)]
        top = jnp.maximum(tops[0], tops[1])
        scales = [jnp.exp(tops[c] - top) for c in range(2)]
        norm = sum(scales[c] * stats[e, c, 1:2, lanes] for c in range(2))
        for c in range(2):
            inverse = scales[c] / norm
            for block in blocks(lanes):
                inverse_norm[e, c, block, :] = turn(inverse[:, block])
        lanes = slice(cut.first, total)
        inverse = 1.0 / stats[e, 0, 1:2, lanes]
        for block, source in zip(blocks(lanes), blocks(slice(0, total - cut.first))):
            inverse_norm[e, 0, block, :] = turn(inverse[:, source])

    def ratios(cut, came):
        e, lanes, rest = cut.e, slice(0, cut.first), slice(cut.first, total)
        below = weights[came, rest, :] * inverse_norm[e, 0, rest, :]
        return [
            jnp.concatenate([weights[came, lanes, :] * inverse_norm[e, c, lanes, :], below], axis=0)
            for c in range(2)
        ]

    def weigh(cut, came, gives):
        e, spans, ranks = cut.e, cut.spans, cut.ranks
        for c, ratio in enumerate(ratios(cut, came)):
            weights[gives, spans[c], :] = nn_dot(kernel_rows[e, spans[c], :], ratio.astype(jnp.bfloat16))

    def move(cut, came):
        e, spans, ranks = cut.e, cut.spans, cut.ranks
        later = rows_of(e, 0, CHIPS).astype(jnp.float32)
        return [
            nn_dot(kernel_rows[e, spans[c], :], (ratio * later).astype(jnp.bfloat16))
            for c, ratio in enumerate(ratios(cut, came))
        ]

    def step_back(cut, came, gives):
        e, spans, ranks = cut.e, cut.spans, cut.ranks
        later = rows_of(e, 0, CHIPS).astype(jnp.float32)
        moved = []
        for c, ratio in enumerate(ratios(cut, came)):
            right = jnp.concatenate(
                [(ratio * later).astype(jnp.bfloat16), ratio.astype(jnp.bfloat16)], axis=1
            )
            both = nn_dot(kernel_rows[e, spans[c], :], right)
            weights[gives, spans[c], :] = both[:, width:]
            moved.append(both[:, :width])
        return moved

    def gradient(cut, moved, gives):
        e, spans, ranks = cut.e, cut.spans, cut.ranks
        part = jnp.zeros((width, width), jnp.float32)
        for c in range(2):
            residual = moved[c] - predicted[e, spans[c], :] * weights[gives, spans[c], :]
            part = part + tn_dot(residual.astype(jnp.bfloat16), columns_of(e, *ranks[c]))
        return part

    def hand_on():
        passes(lambda copy: copy.start(), arrive)
        for slot in range(4, EARLY):
            middle(slot).start()

    pl.when(jnp.logical_and(tm == 1, z == 2))(hand_on)
    for slot in range(1, 4):
        arrive(slot)

        @pl.when(tm == 1)
        def _():
            middle(slot).start()

    @pl.when(tm == 1)
    def _():
        cut = Cut(0, EARLY, EARLY)
        pl.when(z != 2)(hand_on)
        spread_logs(0, EARLY)
        prepare_columns(0, 0, EARLY)
        prepare_rows(0, 0, EARLY)
        tile(cut, 0)
        for slot in range(EARLY, CHIPS):
            arrive(slot)
            middle(slot).start()
        spread_logs(EARLY, CHIPS)
        prepare_columns(0, EARLY, CHIPS)
        prepare_rows(0, EARLY, CHIPS)
        tile(cut, 1)
        tall_tile(cut)
        normalize(cut)
        last = jnp.exp(bias[1] - jnp.max(bias[1], axis=0, keepdims=True))
        weights[1] = last / jnp.sum(last, axis=0, keepdims=True)
        weigh(cut, 1, 0)
        for b, block in enumerate(blocks(slice(0, total))):
            lean[b : b + 1, :] = weights[0, block, :].T[0:1, :]
        lean_copy.start()
        score_mine[...] = gradient(cut, move(cut, 1), 0)

    @pl.when(tm == 0)
    def _():
        zero, one = Cut(0, 4, 4), Cut(1, 4, LANES_ONE)
        spread_logs(0, 4)
        for e in range(2):
            prepare_columns(e, 0, 4)
        prepare_rows(0, 0, 4)
        tile(zero, 0)
        for slot in range(LANES_ONE):
            middle(slot).wait_recv()
        prepare_rows(1, 0, LANES_ONE)
        tile(one, 0)
        for slot in range(4, CHIPS):
            arrive(slot)
        spread_logs(4, CHIPS)
        for e in range(2):
            prepare_columns(e, 4, CHIPS)
        prepare_rows(0, 4, CHIPS)
        tile(zero, 1)
        tall_tile(zero)
        normalize(zero)
        tile(one, 1)
        for slot in range(LANES_ONE, CHIPS):
            middle(slot).wait_recv()
        prepare_rows(1, LANES_ONE, CHIPS)
        tall_tile(one)
        normalize(one)
        lean_copy.wait_recv()
        for b, block in enumerate(blocks(slice(0, total))):
            weights[2, block, :] = turn(lean[b : b + 1, :])
        moved = step_back(one, 2, 1)
        part = gradient(one, moved, 1)
        moved = step_back(zero, 1, 0)
        score_mine[...] = part + gradient(zero, moved, 0)

    score_copy.start()
    for k in range(2):
        smoothed_ref[k : k + 1, :] = weights[k, 0:rows, :].T[0:1, :] * total
    score_copy.wait_recv()
    score_ref[...] = (score_mine[...] + score_theirs[...]) * p_down

    for d in range(4):

        @pl.when(z != d)
        def _():
            for q in range(2):

                @pl.when(sends_to(d, q))
                def _():
                    for copy in own(slot_of(d, q), 2 * d + q):
                        copy.wait_send()

    for copy in own(1, across):
        copy.wait_send()
    score_copy.wait_send()

    @pl.when(tm == 1)
    def _():
        passes(lambda copy: copy.wait_send(), lambda slot: None)
        for slot in range(CHIPS):
            middle(slot).wait_send()
        lean_copy.wait_send()


def hand_over(a_in, b_in, a_out, b_out, sems):
    leaving = [
        pltpu.make_async_copy(a_in, a_out, sems.at[0]),
        pltpu.make_async_copy(b_in, b_out, sems.at[1]),
    ]
    for copy in leaving:
        copy.start()
    for copy in leaving:
        copy.wait()


def fused(particles, log_weight, trans_weight, precision):
    steps_here, rows, width = particles.shape
    total = CHIPS * rows
    whole = pl.BlockSpec(memory_space=pltpu.VMEM)
    arguments = (
        particles.reshape(steps_here * rows, width), log_weight, trans_weight, precision.reshape(1, width)
    )
    smoothed, score = pl.pallas_call(
        smoother_kernel,
        out_shape=(
            pltpu.VMEM((steps_here, rows), jnp.float32),
            pltpu.VMEM((width, width), jnp.float32),
        ),
        in_specs=[pl.BlockSpec(memory_space=pltpu.HBM)] * 4,
        out_specs=(whole, whole),
        scratch_shapes=[
            pltpu.VMEM((CHIPS, steps_here, rows), jnp.float32),
            pltpu.VMEM((width, width), jnp.bfloat16),
            pltpu.VMEM((1, width), jnp.float32),
            pltpu.VMEM((CHIPS, 2 * rows, width), jnp.bfloat16),
            pltpu.VMEM((CHIPS, rows, width), jnp.bfloat16),
            pltpu.VMEM((2, total, total), jnp.bfloat16),
            pltpu.VMEM((2, 2, 8, total), jnp.float32),
            pltpu.VMEM((2, 2, total, width), jnp.float32),
            pltpu.VMEM((2, total, width), jnp.float32),
            pltpu.VMEM((2, total, width), jnp.bfloat16),
            pltpu.VMEM((2, total, width), jnp.float32),
            pltpu.VMEM((3, total, width), jnp.float32),
            pltpu.VMEM((CHIPS, EXTRA, width), jnp.float32),
            pltpu.VMEM((8, width), jnp.float32),
            pltpu.VMEM((width, width), jnp.float32),
            pltpu.VMEM((width, width), jnp.float32),
            pltpu.SemaphoreType.DMA((4,)),
            pltpu.SemaphoreType.DMA((2 * CHIPS,)),
            pltpu.SemaphoreType.DMA((2 * CHIPS,)),
            pltpu.SemaphoreType.DMA((CHIPS + 2,)),
            pltpu.SemaphoreType.DMA((CHIPS,)),
            pltpu.SemaphoreType.DMA((CHIPS,)),
            pltpu.SemaphoreType.DMA((CHIPS,)),
            pltpu.SemaphoreType.DMA((2,)),
            pltpu.SemaphoreType.REGULAR((CHIPS,)),
        ],
        compiler_params=pltpu.CompilerParams(
            collective_id=0, has_side_effects=True, vmem_limit_bytes=40 * 2**20
        ),
    )(*[pltpu.with_memory_space_constraint(a, pltpu.HBM) for a in arguments])
    return pl.pallas_call(
        hand_over,
        out_shape=(
            jax.ShapeDtypeStruct((steps_here, rows), jnp.float32),
            jax.ShapeDtypeStruct((width, width), jnp.float32),
        ),
        in_specs=[whole] * 2,
        out_specs=(pl.BlockSpec(memory_space=pltpu.HBM),) * 2,
        scratch_shapes=[
            pltpu.SemaphoreType.DMA((2,)),
        ],
        compiler_params=pltpu.CompilerParams(vmem_limit_bytes=40 * 2**20),
    )(smoothed, score)


def plan(particles, log_weight, trans_weight, precision):
    steps_here, rows, width = particles.shape
    n_dom = lax.axis_size("dom")
    total = n_dom * rows
    small = total <= MOST_ROWS and total % (2 * width) == 0 and rows <= width and rows % 16 == 0
    shaped = n_dom == 8 and lax.axis_size("tm") == 2 and steps_here == 2 and width == 128
    if small and shaped:
        return fused(particles, log_weight, trans_weight, precision)
    return shards(particles, log_weight, trans_weight, precision)


def solution(mesh):
    placed = (P("tm", ("seq", "dom"), None), P("tm", ("seq", "dom")), P(), P())
    return jax.shard_map(
        plan,
        mesh=mesh,
        in_specs=placed,
        out_specs=(P("tm", ("seq", "dom")), P("seq", None)),
        check_vma=False,
    )
```

```python
import functools

import jax
import jax.numpy as jnp
from jax import lax
from jax.experimental import pallas as pl
from jax.experimental.pallas import tpu as pltpu
from jax.sharding import PartitionSpec as P

exact_mode = lax.Precision.HIGHEST


def from_behind(x, axis, by):
    size = lax.axis_size(axis)
    pairs = [(i, i + by) for i in range(size) if 0 <= i + by < size]
    return lax.ppermute(x, axis, pairs)


def block_size(length):
    best = 1
    for trial in range(1, min(length, 512) + 1):
        if length % trial == 0:
            best = trial
    return best


def project_rows(rows, precision, weight_full):
    return jnp.dot(rows.astype(jnp.float32) * precision, weight_full, precision=exact_mode).astype(
        jnp.bfloat16
    )


def pair_scores(row_proj, column_rows, column_bias):
    return (
        jnp.einsum("id,jd->ij", row_proj, column_rows, preferred_element_type=jnp.float32)
        + column_bias[None, :]
    )


def make_norm_fold(row_proj, bias_row, carried, block_in, first_row):
    length = block_in.shape[0]
    size = block_size(length)

    def inner(position, state):
        row_top, row_total = state
        offset = position * size
        column_rows = lax.dynamic_slice_in_dim(block_in, offset, size, 0)
        bias_part = lax.dynamic_slice_in_dim(bias_row, first_row + offset, size, 0)
        scores = pair_scores(row_proj, column_rows, bias_part)
        new_top = jnp.maximum(row_top, jnp.max(scores, axis=1))
        row_total = row_total * jnp.exp(row_top - new_top) + jnp.sum(
            jnp.exp(scores - new_top[:, None]), axis=1
        )
        return (new_top, row_total)

    return lax.fori_loop(0, length // size, inner, carried)


def make_column_fold(row_proj, bias_row, row_norm, row_weight, carried, block_in, first_row):
    length = block_in.shape[0]
    size = block_size(length)

    def inner(position, state):
        moved, column_sums = state
        offset = position * size
        column_rows = lax.dynamic_slice_in_dim(block_in, offset, size, 0)
        bias_part = lax.dynamic_slice_in_dim(bias_row, first_row + offset, size, 0)
        scores = pair_scores(row_proj, column_rows, bias_part)
        backward = (row_weight[:, None] * jnp.exp(scores - row_norm[:, None])).astype(jnp.bfloat16)
        moved = moved + jnp.dot(backward, column_rows, preferred_element_type=jnp.float32)
        column_sums = lax.dynamic_update_slice_in_dim(
            column_sums, jnp.sum(backward.astype(jnp.float32), axis=0), first_row + offset, 0
        )
        return (moved, column_sums)

    return lax.fori_loop(0, length // size, inner, carried)


def shards(particles, log_weight, trans_weight, precision):
    steps_here, rows_here, width = particles.shape
    tm_count = lax.axis_size("tm")
    dom_count = lax.axis_size("dom")
    total_rows = rows_here * dom_count
    tm_place = lax.axis_index("tm")
    is_last = tm_place == tm_count - 1
    weight_full = trans_weight.astype(jnp.float32)
    boundary = from_behind(particles[0], "tm", -1)
    later_sets = [particles[1]] + [boundary]
    later_proj = [project_rows(rows, precision, weight_full) for rows in later_sets]
    biases = []
    for k in range(steps_here):
        predicted = jnp.dot(particles[k], trans_weight.T, preferred_element_type=jnp.float32)
        biases.append(log_weight[k] - 0.5 * jnp.sum(precision * predicted * predicted, axis=1))
    local_bias = jnp.stack(biases)
    full_bias = lax.all_gather(local_bias, "dom", axis=1, tiled=True)
    row_norms = []
    whole = lax.all_gather(particles, "dom", axis=1, tiled=True)
    for k in range(steps_here):
        start_state = (
            jnp.full((rows_here,), -jnp.inf, jnp.float32),
            jnp.zeros((rows_here,), jnp.float32),
        )
        row_top, row_total = make_norm_fold(later_proj[k], full_bias[k], start_state, whole[k], 0)
        row_norms.append(row_top + jnp.log(row_total))
    final_logs = log_weight[steps_here - 1]
    global_top = lax.pmax(jnp.max(final_logs), "dom")
    global_total = lax.psum(jnp.sum(jnp.exp(final_logs - global_top)), "dom")
    final_weights = jnp.exp(final_logs - global_top) / global_total
    carried = (
        jnp.zeros((steps_here, rows_here), jnp.float32),
        jnp.zeros((width, width), jnp.float32),
    )
    for r in range(tm_count):
        if r == 0:
            incoming = jnp.zeros((rows_here,), jnp.float32)
        else:
            incoming = from_behind(carried[0][0], "tm", -1)
        owner = tm_count - 1 - r
        backward_partial_value = jnp.zeros((width, width), jnp.float32)
        outputs = [None] * steps_here
        row_weight = incoming
        for backward_k in range(steps_here - 1, -1, -1):
            column_rows = particles[backward_k]
            backward_start_state = (
                jnp.zeros((rows_here, width), jnp.float32),
                jnp.zeros((total_rows,), jnp.float32),
            )
            moved, column_sums = make_column_fold(
                later_proj[backward_k],
                full_bias[backward_k],
                row_norms[backward_k],
                row_weight,
                backward_start_state,
                whole[backward_k],
                0,
            )
            column_weights = lax.psum_scatter(column_sums, "dom", scatter_dimension=0, tiled=True)
            outer = jnp.dot(
                later_sets[backward_k].astype(jnp.float32).T, moved, precision=exact_mode
            )
            column_float = column_rows.astype(jnp.float32)
            moment = jnp.dot(
                column_float.T * column_weights[None, :], column_float, precision=exact_mode
            )
            backward_partial_value = backward_partial_value + precision[:, None] * (
                outer - jnp.dot(weight_full, moment, precision=exact_mode)
            )
            if backward_k == steps_here - 1:
                column_weights = jnp.where(is_last, final_weights, column_weights)
            outputs[backward_k] = column_weights
            row_weight = column_weights
        is_owner = tm_place == owner
        carried = (
            jnp.where(is_owner, jnp.stack(outputs), carried[0]),
            jnp.where(is_owner, backward_partial_value, carried[1]),
        )
    stacked, partial_value = carried
    score = lax.psum(partial_value, ("dom", "tm"))
    return (stacked * total_rows, score)


MESH = pl.DeviceIdType.MESH
EXTRA = 16
CHIPS = 8
EARLY = 6
LANES_ONE = 6
MOST_ROWS = 1024


def nt_dot(a, b):
    return lax.dot_general(a, b, (((1,), (1,)), ((), ())), preferred_element_type=jnp.float32)


def tn_dot(a, b):
    return lax.dot_general(a, b, (((0,), (0,)), ((), ())), preferred_element_type=jnp.float32)


def nn_dot(a, b):
    return jnp.dot(a, b, preferred_element_type=jnp.float32)


def split_three(x):
    high = x.astype(jnp.bfloat16)
    rest = x - high.astype(jnp.float32)
    middle = rest.astype(jnp.bfloat16)
    low = (rest - middle.astype(jnp.float32)).astype(jnp.bfloat16)
    return high, middle, low


def smoother_kernel(
    x_hbm, lw_hbm, w_hbm, p_hbm, smoothed_ref, score_ref,
    lw_held, w_ref, p_ref, held, middle_rows, kernel_rows, stats, inverse_norm, bias, projected, predicted,
    weights, stage, lean, score_mine, score_theirs,
    in_sem, send_sem, lw_send_sem, inside_send_sem, recv_sem, lw_sem, inside_sem, late_sem, up_sem,
):
    width = x_hbm.shape[1]
    rows = x_hbm.shape[0] // 2
    total = CHIPS * rows
    dom = lax.axis_index("dom")
    tm = lax.axis_index("tm")
    z, side = dom // 2, dom % 2
    across = dom + 1 - 2 * side
    other = 1 - tm

    def slot_of(d, q):
        high, low, turned = [
            here + there - 2 * here * there for here, there in ((z // 2, d // 2), (z % 2, d % 2), (side, q))
        ]
        return 4 * high + 2 * low + turned + tm * high * (turned - low)

    loads = [
        pltpu.make_async_copy(source, target, in_sem.at[i])
        for i, (source, target) in enumerate(
            [(lw_hbm, lw_held.at[0]), (w_hbm, w_ref), (p_hbm, p_ref), (x_hbm, held.at[0])]
        )
    ]
    barrier = pltpu.get_barrier_semaphore()

    def signal(sem, to_dom, to_tm):
        pl.semaphore_signal(sem, inc=1, device_id={"dom": to_dom, "tm": to_tm}, device_id_type=MESH)

    for d in range(1, 4):

        @pl.when(z < d)
        def _():
            for q in range(2):
                signal(barrier, 2 * d + q, tm)

    signal(barrier, across, tm)
    signal(barrier, dom, other)

    def remote(source, target, send, recv, to_dom, to_tm):
        return pltpu.make_async_remote_copy(
            src_ref=source,
            dst_ref=target,
            send_sem=send,
            recv_sem=recv,
            device_id={"dom": to_dom, "tm": to_tm},
            device_id_type=MESH,
        )

    def own(slot, to_dom):
        return (
            remote(lw_hbm, lw_held.at[slot], lw_send_sem.at[slot], lw_sem.at[slot], to_dom, tm),
            remote(x_hbm, held.at[slot], send_sem.at[slot], recv_sem.at[slot], to_dom, tm),
        )

    def start_own(d, q):
        def start():
            for copy in own(slot_of(d, q), 2 * d + q):
                copy.start()

        pl.when(sends_to(d, q))(start)

    def sends_to(d, q):
        crossed = side == q
        if d == 3:
            crossed = jnp.logical_and(crossed, z != 1)
        return jnp.logical_or(jnp.logical_or(z // 2 == d // 2, tm == 0), crossed)

    near = 2 * (z + 1 - 2 * (z % 2)) + side
    corner = 2 * (z + 1 - 2 * (z % 2)) + 1 - side

    def pass_on(source, slot, to_dom):
        index = CHIPS + 4 * (source - 4) + slot - 4
        return (
            remote(lw_held.at[source], lw_held.at[slot], lw_send_sem.at[index], lw_sem.at[slot], to_dom, tm),
            remote(held.at[source], held.at[slot], send_sem.at[index], recv_sem.at[slot], to_dom, tm),
        )

    def passes(do, ready):
        def run(source, *ways):
            ready(source)
            for slot, to_dom in ways:
                for copy in pass_on(source, slot, to_dom):
                    do(copy)

        @pl.when(z < 2)
        def _():
            run(4, (6, across))
            run(5, (7, across))

        @pl.when(z == 2)
        def _():
            run(5, (4, near), (6, corner), (7, across))
            run(4, (6, across))

        @pl.when(z == 3)
        def _():
            run(5, (7, across))
            ready(4)

    def middle(slot):
        source = x_hbm if slot == 0 else held.at[slot]
        return remote(
            source.at[0:rows], middle_rows.at[slot], inside_send_sem.at[slot], inside_sem.at[slot], dom, other
        )

    lean_copy = remote(lean, lean, inside_send_sem.at[CHIPS], late_sem.at[0], dom, other)
    score_copy = remote(score_mine, score_theirs, inside_send_sem.at[CHIPS + 1], late_sem.at[1], dom, other)

    pl.semaphore_wait(barrier, 2 + 2 * z)
    for d in range(3):

        @pl.when(z > d)
        def _():
            for q in range(2):
                signal(up_sem.at[slot_of(d, q)], 2 * d + q, tm)

    for d, turn_of in ((0, tm >= 0), (1, tm == 1), (2, tm >= 0), (1, tm == 0)):

        @pl.when(jnp.logical_and(z > d, turn_of))
        def _():
            for q in range(2):
                start_own(d, q)

    for copy in own(1, across):
        copy.start()

    @pl.when(tm == 1)
    def _():
        middle(0).start()

    for load in loads:
        load.start()

    for d in range(1, 4):

        @pl.when(z < d)
        def _():
            for q in range(2):
                pl.semaphore_wait(up_sem.at[slot_of(d, q)], 1)
                start_own(d, q)

    stage[...] = jnp.zeros_like(stage)
    for load in loads:
        load.wait()

    def arrive(slot):
        for copy in own(slot, across):
            copy.wait_recv()

    weight = w_ref[...]
    p_row = p_ref[...]
    p_down = jnp.broadcast_to(p_row, (width, width)).T
    scaled = jnp.concatenate(split_three(p_down * weight.astype(jnp.float32)), axis=1)
    line = lax.broadcasted_iota(jnp.int32, (EXTRA, 2 * width), 0)
    which = lax.broadcasted_iota(jnp.int32, (EXTRA, 2 * width), 1) // width
    pick = jnp.where((line < 6) & (line % 2 == which), 1.0, 0.0).astype(jnp.bfloat16)

    def flat(block):
        return block.reshape(block.shape[0] * rows, width)

    def columns_of(e, first, last):
        return flat(held[first:last, e * rows : (e + 1) * rows, :])

    def rows_of(e, first, last):
        return flat(middle_rows[first:last] if e else held[first:last, rows:, :])

    def spread_logs(first, last):
        for r in range(first, last):
            for n, value in enumerate(split_three(lw_held[r])):
                stage[2 * n : 2 * n + 2, r * width : r * width + rows] = value.astype(jnp.float32)
        spread = tn_dot(stage[:, first * width : last * width].astype(jnp.bfloat16), pick)
        for r in range(first, last):
            at = (r - first) * width
            for e in range(2):
                bias[e, r * rows : (r + 1) * rows, :] = spread[at : at + rows, e * width : (e + 1) * width]

    def prepare_columns(e, first, last):
        span = slice(first * rows, last * rows)
        mean = nt_dot(columns_of(e, first, last), weight)
        predicted[e, span, :] = mean
        energy = jnp.sum(p_row * mean * mean, axis=1, keepdims=True)
        bias[e, span, :] = bias[e, span, :] - 0.5 * energy

    def prepare_rows(e, first, last):
        wide = nn_dot(rows_of(e, first, last), scaled)
        projected[e, first * rows : last * rows, :] = (
            wide[:, :width] + (wide[:, width : 2 * width] + wide[:, 2 * width :])
        ).astype(jnp.bfloat16)

    class Cut:
        def __init__(self, e, columns, lanes):
            self.e, self.first = e, lanes * rows // width * width
            self.ranks = ((0, columns), (columns, CHIPS))
            self.spans = [slice(a * rows, b * rows) for a, b in self.ranks]

    def exponentials(e, first, last, lanes):
        span = slice(first * rows, last * rows)
        scores = nt_dot(columns_of(e, first, last), projected[e, lanes, :])
        scores = scores + jnp.concatenate([bias[e, span, :]] * ((lanes.stop - lanes.start) // width), axis=1)
        top = jnp.max(scores, axis=0, keepdims=True)
        terms = jnp.exp(scores - top)
        kernel_rows[e, span, lanes] = terms.astype(jnp.bfloat16)
        return top, jnp.sum(terms, axis=0, keepdims=True)

    def tile(cut, c):
        e, lanes = cut.e, slice(0, cut.first)
        top, norm = exponentials(e, *cut.ranks[c], lanes)
        stats[e, c, 0:1, lanes] = top
        stats[e, c, 1:2, lanes] = norm

    def tall_tile(cut):
        e, lanes = cut.e, slice(cut.first, total)
        top, norm = exponentials(e, 0, CHIPS, lanes)
        stats[e, 0, 0:1, lanes] = top
        stats[e, 0, 1:2, lanes] = norm

    def turn(row):
        return jnp.broadcast_to(row, (width, width)).T

    def blocks(lanes):
        return [slice(at, at + width) for at in range(lanes.start, lanes.stop, width)]

    def normalize(cut):
        e, lanes = cut.e, slice(0, cut.first)
        tops = [stats[e, c, 0:1, lanes] for c in range(2)]
        top = jnp.maximum(tops[0], tops[1])
        scales = [jnp.exp(tops[c] - top) for c in range(2)]
        norm = sum(scales[c] * stats[e, c, 1:2, lanes] for c in range(2))
        for c in range(2):
            inverse = scales[c] / norm
            for block in blocks(lanes):
                inverse_norm[e, c, block, :] = turn(inverse[:, block])
        lanes = slice(cut.first, total)
        inverse = 1.0 / stats[e, 0, 1:2, lanes]
        for block, source in zip(blocks(lanes), blocks(slice(0, total - cut.first))):
            inverse_norm[e, 0, block, :] = turn(inverse[:, source])

    def ratios(cut, came):
        e, lanes, rest = cut.e, slice(0, cut.first), slice(cut.first, total)
        below = weights[came, rest, :] * inverse_norm[e, 0, rest, :]
        return [
            jnp.concatenate([weights[came, lanes, :] * inverse_norm[e, c, lanes, :], below], axis=0)
            for c in range(2)
        ]

    def weigh(cut, came, gives):
        e, spans, ranks = cut.e, cut.spans, cut.ranks
        for c, ratio in enumerate(ratios(cut, came)):
            weights[gives, spans[c], :] = nn_dot(kernel_rows[e, spans[c], :], ratio.astype(jnp.bfloat16))

    def move(cut, came):
        e, spans, ranks = cut.e, cut.spans, cut.ranks
        later = rows_of(e, 0, CHIPS).astype(jnp.float32)
        return [
            nn_dot(kernel_rows[e, spans[c], :], (ratio * later).astype(jnp.bfloat16))
            for c, ratio in enumerate(ratios(cut, came))
        ]

    def step_back(cut, came, gives):
        e, spans, ranks = cut.e, cut.spans, cut.ranks
        later = rows_of(e, 0, CHIPS).astype(jnp.float32)
        moved = []
        for c, ratio in enumerate(ratios(cut, came)):
            right = jnp.concatenate(
                [(ratio * later).astype(jnp.bfloat16), ratio.astype(jnp.bfloat16)], axis=1
            )
            both = nn_dot(kernel_rows[e, spans[c], :], right)
            weights[gives, spans[c], :] = both[:, width:]
            moved.append(both[:, :width])
        return moved

    def gradient(cut, moved, gives):
        e, spans, ranks = cut.e, cut.spans, cut.ranks
        part = jnp.zeros((width, width), jnp.float32)
        for c in range(2):
            residual = moved[c] - predicted[e, spans[c], :] * weights[gives, spans[c], :]
            part = part + tn_dot(residual.astype(jnp.bfloat16), columns_of(e, *ranks[c]))
        return part

    def hand_on():
        passes(lambda copy: copy.start(), arrive)
        for slot in range(4, EARLY):
            middle(slot).start()

    pl.when(jnp.logical_and(tm == 1, z == 2))(hand_on)
    for slot in range(1, 4):
        arrive(slot)

        @pl.when(tm == 1)
        def _():
            middle(slot).start()

    @pl.when(tm == 1)
    def _():
        cut = Cut(0, EARLY, EARLY)
        pl.when(z != 2)(hand_on)
        spread_logs(0, EARLY)
        prepare_columns(0, 0, EARLY)
        prepare_rows(0, 0, EARLY)
        tile(cut, 0)
        for slot in range(EARLY, CHIPS):
            arrive(slot)
            middle(slot).start()
        spread_logs(EARLY, CHIPS)
        prepare_columns(0, EARLY, CHIPS)
        prepare_rows(0, EARLY, CHIPS)
        tile(cut, 1)
        tall_tile(cut)
        normalize(cut)
        last = jnp.exp(bias[1] - jnp.max(bias[1], axis=0, keepdims=True))
        weights[1] = last / jnp.sum(last, axis=0, keepdims=True)
        weigh(cut, 1, 0)
        for b, block in enumerate(blocks(slice(0, total))):
            lean[b : b + 1, :] = weights[0, block, :].T[0:1, :]
        lean_copy.start()
        score_mine[...] = gradient(cut, move(cut, 1), 0)

    @pl.when(tm == 0)
    def _():
        zero, one = Cut(0, 4, 4), Cut(1, 4, LANES_ONE)
        spread_logs(0, 4)
        for e in range(2):
            prepare_columns(e, 0, 4)
        prepare_rows(0, 0, 4)
        tile(zero, 0)
        for slot in range(LANES_ONE):
            middle(slot).wait_recv()
        prepare_rows(1, 0, LANES_ONE)
        tile(one, 0)
        for slot in range(4, CHIPS):
            arrive(slot)
        spread_logs(4, CHIPS)
        for e in range(2):
            prepare_columns(e, 4, CHIPS)
        prepare_rows(0, 4, CHIPS)
        tile(one, 1)
        tile(zero, 1)
        for slot in range(LANES_ONE, CHIPS):
            middle(slot).wait_recv()
        prepare_rows(1, LANES_ONE, CHIPS)
        tall_tile(one)
        tall_tile(zero)
        normalize(one)
        normalize(zero)
        lean_copy.wait_recv()
        for b, block in enumerate(blocks(slice(0, total))):
            weights[2, block, :] = turn(lean[b : b + 1, :])
        moved = step_back(one, 2, 1)
        part = gradient(one, moved, 1)
        moved = step_back(zero, 1, 0)
        score_mine[...] = part + gradient(zero, moved, 0)

    score_copy.start()
    for k in range(2):
        smoothed_ref[k : k + 1, :] = weights[k, 0:rows, :].T[0:1, :] * total
    score_copy.wait_recv()
    score_ref[...] = (score_mine[...] + score_theirs[...]) * p_down

    for d in range(4):

        @pl.when(z != d)
        def _():
            for q in range(2):

                @pl.when(sends_to(d, q))
                def _():
                    for copy in own(slot_of(d, q), 2 * d + q):
                        copy.wait_send()

    for copy in own(1, across):
        copy.wait_send()
    score_copy.wait_send()

    @pl.when(tm == 1)
    def _():
        passes(lambda copy: copy.wait_send(), lambda slot: None)
        for slot in range(CHIPS):
            middle(slot).wait_send()
        lean_copy.wait_send()


def hand_over(a_in, b_in, a_out, b_out, sems):
    leaving = [
        pltpu.make_async_copy(a_in, a_out, sems.at[0]),
        pltpu.make_async_copy(b_in, b_out, sems.at[1]),
    ]
    for copy in leaving:
        copy.start()
    for copy in leaving:
        copy.wait()


def fused(particles, log_weight, trans_weight, precision):
    steps_here, rows, width = particles.shape
    total = CHIPS * rows
    whole = pl.BlockSpec(memory_space=pltpu.VMEM)
    arguments = (
        particles.reshape(steps_here * rows, width), log_weight, trans_weight, precision.reshape(1, width)
    )
    smoothed, score = pl.pallas_call(
        smoother_kernel,
        out_shape=(
            pltpu.VMEM((steps_here, rows), jnp.float32),
            pltpu.VMEM((width, width), jnp.float32),
        ),
        in_specs=[pl.BlockSpec(memory_space=pltpu.HBM)] * 4,
        out_specs=(whole, whole),
        scratch_shapes=[
            pltpu.VMEM((CHIPS, steps_here, rows), jnp.float32),
            pltpu.VMEM((width, width), jnp.bfloat16),
            pltpu.VMEM((1, width), jnp.float32),
            pltpu.VMEM((CHIPS, 2 * rows, width), jnp.bfloat16),
            pltpu.VMEM((CHIPS, rows, width), jnp.bfloat16),
            pltpu.VMEM((2, total, total), jnp.bfloat16),
            pltpu.VMEM((2, 2, 8, total), jnp.float32),
            pltpu.VMEM((2, 2, total, width), jnp.float32),
            pltpu.VMEM((2, total, width), jnp.float32),
            pltpu.VMEM((2, total, width), jnp.bfloat16),
            pltpu.VMEM((2, total, width), jnp.float32),
            pltpu.VMEM((3, total, width), jnp.float32),
            pltpu.VMEM((EXTRA, CHIPS * width), jnp.float32),
            pltpu.VMEM((8, width), jnp.float32),
            pltpu.VMEM((width, width), jnp.float32),
            pltpu.VMEM((width, width), jnp.float32),
            pltpu.SemaphoreType.DMA((4,)),
            pltpu.SemaphoreType.DMA((2 * CHIPS,)),
            pltpu.SemaphoreType.DMA((2 * CHIPS,)),
            pltpu.SemaphoreType.DMA((CHIPS + 2,)),
            pltpu.SemaphoreType.DMA((CHIPS,)),
            pltpu.SemaphoreType.DMA((CHIPS,)),
            pltpu.SemaphoreType.DMA((CHIPS,)),
            pltpu.SemaphoreType.DMA((2,)),
            pltpu.SemaphoreType.REGULAR((CHIPS,)),
        ],
        compiler_params=pltpu.CompilerParams(
            collective_id=0, has_side_effects=True, vmem_limit_bytes=40 * 2**20
        ),
    )(*[pltpu.with_memory_space_constraint(a, pltpu.HBM) for a in arguments])
    return pl.pallas_call(
        hand_over,
        out_shape=(
            jax.ShapeDtypeStruct((steps_here, rows), jnp.float32),
            jax.ShapeDtypeStruct((width, width), jnp.float32),
        ),
        in_specs=[whole] * 2,
        out_specs=(pl.BlockSpec(memory_space=pltpu.HBM),) * 2,
        scratch_shapes=[
            pltpu.SemaphoreType.DMA((2,)),
        ],
        compiler_params=pltpu.CompilerParams(vmem_limit_bytes=40 * 2**20),
    )(smoothed, score)


def plan(particles, log_weight, trans_weight, precision):
    steps_here, rows, width = particles.shape
    n_dom = lax.axis_size("dom")
    total = n_dom * rows
    small = total <= MOST_ROWS and total % (2 * width) == 0 and rows <= width and rows % 16 == 0
    shaped = n_dom == 8 and lax.axis_size("tm") == 2 and steps_here == 2 and width == 128
    if small and shaped:
        return fused(particles, log_weight, trans_weight, precision)
    return shards(particles, log_weight, trans_weight, precision)


def solution(mesh):
    placed = (P("tm", ("seq", "dom"), None), P("tm", ("seq", "dom")), P(), P())
    return jax.shard_map(
        plan,
        mesh=mesh,
        in_specs=placed,
        out_specs=(P("tm", ("seq", "dom")), P("seq", None)),
        check_vma=False,
    )
```

```python
import functools

import jax
import jax.numpy as jnp
from jax import lax
from jax.experimental import pallas as pl
from jax.experimental.pallas import tpu as pltpu
from jax.sharding import PartitionSpec as P

exact_mode = lax.Precision.HIGHEST


def from_behind(x, axis, by):
    size = lax.axis_size(axis)
    pairs = [(i, i + by) for i in range(size) if 0 <= i + by < size]
    return lax.ppermute(x, axis, pairs)


def block_size(length):
    best = 1
    for trial in range(1, min(length, 512) + 1):
        if length % trial == 0:
            best = trial
    return best


def project_rows(rows, precision, weight_full):
    return jnp.dot(rows.astype(jnp.float32) * precision, weight_full, precision=exact_mode).astype(
        jnp.bfloat16
    )


def pair_scores(row_proj, column_rows, column_bias):
    return (
        jnp.einsum("id,jd->ij", row_proj, column_rows, preferred_element_type=jnp.float32)
        + column_bias[None, :]
    )


def make_norm_fold(row_proj, bias_row, carried, block_in, first_row):
    length = block_in.shape[0]
    size = block_size(length)

    def inner(position, state):
        row_top, row_total = state
        offset = position * size
        column_rows = lax.dynamic_slice_in_dim(block_in, offset, size, 0)
        bias_part = lax.dynamic_slice_in_dim(bias_row, first_row + offset, size, 0)
        scores = pair_scores(row_proj, column_rows, bias_part)
        new_top = jnp.maximum(row_top, jnp.max(scores, axis=1))
        row_total = row_total * jnp.exp(row_top - new_top) + jnp.sum(
            jnp.exp(scores - new_top[:, None]), axis=1
        )
        return (new_top, row_total)

    return lax.fori_loop(0, length // size, inner, carried)


def make_column_fold(row_proj, bias_row, row_norm, row_weight, carried, block_in, first_row):
    length = block_in.shape[0]
    size = block_size(length)

    def inner(position, state):
        moved, column_sums = state
        offset = position * size
        column_rows = lax.dynamic_slice_in_dim(block_in, offset, size, 0)
        bias_part = lax.dynamic_slice_in_dim(bias_row, first_row + offset, size, 0)
        scores = pair_scores(row_proj, column_rows, bias_part)
        backward = (row_weight[:, None] * jnp.exp(scores - row_norm[:, None])).astype(jnp.bfloat16)
        moved = moved + jnp.dot(backward, column_rows, preferred_element_type=jnp.float32)
        column_sums = lax.dynamic_update_slice_in_dim(
            column_sums, jnp.sum(backward.astype(jnp.float32), axis=0), first_row + offset, 0
        )
        return (moved, column_sums)

    return lax.fori_loop(0, length // size, inner, carried)


def shards(particles, log_weight, trans_weight, precision):
    steps_here, rows_here, width = particles.shape
    tm_count = lax.axis_size("tm")
    dom_count = lax.axis_size("dom")
    total_rows = rows_here * dom_count
    tm_place = lax.axis_index("tm")
    is_last = tm_place == tm_count - 1
    weight_full = trans_weight.astype(jnp.float32)
    boundary = from_behind(particles[0], "tm", -1)
    later_sets = [particles[1]] + [boundary]
    later_proj = [project_rows(rows, precision, weight_full) for rows in later_sets]
    biases = []
    for k in range(steps_here):
        predicted = jnp.dot(particles[k], trans_weight.T, preferred_element_type=jnp.float32)
        biases.append(log_weight[k] - 0.5 * jnp.sum(precision * predicted * predicted, axis=1))
    local_bias = jnp.stack(biases)
    full_bias = lax.all_gather(local_bias, "dom", axis=1, tiled=True)
    row_norms = []
    whole = lax.all_gather(particles, "dom", axis=1, tiled=True)
    for k in range(steps_here):
        start_state = (
            jnp.full((rows_here,), -jnp.inf, jnp.float32),
            jnp.zeros((rows_here,), jnp.float32),
        )
        row_top, row_total = make_norm_fold(later_proj[k], full_bias[k], start_state, whole[k], 0)
        row_norms.append(row_top + jnp.log(row_total))
    final_logs = log_weight[steps_here - 1]
    global_top = lax.pmax(jnp.max(final_logs), "dom")
    global_total = lax.psum(jnp.sum(jnp.exp(final_logs - global_top)), "dom")
    final_weights = jnp.exp(final_logs - global_top) / global_total
    carried = (
        jnp.zeros((steps_here, rows_here), jnp.float32),
        jnp.zeros((width, width), jnp.float32),
    )
    for r in range(tm_count):
        if r == 0:
            incoming = jnp.zeros((rows_here,), jnp.float32)
        else:
            incoming = from_behind(carried[0][0], "tm", -1)
        owner = tm_count - 1 - r
        backward_partial_value = jnp.zeros((width, width), jnp.float32)
        outputs = [None] * steps_here
        row_weight = incoming
        for backward_k in range(steps_here - 1, -1, -1):
            column_rows = particles[backward_k]
            backward_start_state = (
                jnp.zeros((rows_here, width), jnp.float32),
                jnp.zeros((total_rows,), jnp.float32),
            )
            moved, column_sums = make_column_fold(
                later_proj[backward_k],
                full_bias[backward_k],
                row_norms[backward_k],
                row_weight,
                backward_start_state,
                whole[backward_k],
                0,
            )
            column_weights = lax.psum_scatter(column_sums, "dom", scatter_dimension=0, tiled=True)
            outer = jnp.dot(
                later_sets[backward_k].astype(jnp.float32).T, moved, precision=exact_mode
            )
            column_float = column_rows.astype(jnp.float32)
            moment = jnp.dot(
                column_float.T * column_weights[None, :], column_float, precision=exact_mode
            )
            backward_partial_value = backward_partial_value + precision[:, None] * (
                outer - jnp.dot(weight_full, moment, precision=exact_mode)
            )
            if backward_k == steps_here - 1:
                column_weights = jnp.where(is_last, final_weights, column_weights)
            outputs[backward_k] = column_weights
            row_weight = column_weights
        is_owner = tm_place == owner
        carried = (
            jnp.where(is_owner, jnp.stack(outputs), carried[0]),
            jnp.where(is_owner, backward_partial_value, carried[1]),
        )
    stacked, partial_value = carried
    score = lax.psum(partial_value, ("dom", "tm"))
    return (stacked * total_rows, score)


MESH = pl.DeviceIdType.MESH
EXTRA = 16
CHIPS = 8
EARLY = 6
LANES_ONE = 6
MOST_ROWS = 1024


def nt_dot(a, b):
    return lax.dot_general(a, b, (((1,), (1,)), ((), ())), preferred_element_type=jnp.float32)


def tn_dot(a, b):
    return lax.dot_general(a, b, (((0,), (0,)), ((), ())), preferred_element_type=jnp.float32)


def nn_dot(a, b):
    return jnp.dot(a, b, preferred_element_type=jnp.float32)


def split_three(x):
    high = x.astype(jnp.bfloat16)
    rest = x - high.astype(jnp.float32)
    middle = rest.astype(jnp.bfloat16)
    low = (rest - middle.astype(jnp.float32)).astype(jnp.bfloat16)
    return high, middle, low


def smoother_kernel(
    x_hbm, lw_hbm, w_hbm, p_hbm, smoothed_ref, score_ref,
    lw_held, w_ref, p_ref, held, middle_rows, kernel_rows, stats, inverse_norm, bias, projected, predicted,
    weights, stage, lean, score_mine, score_theirs,
    in_sem, send_sem, lw_send_sem, inside_send_sem, recv_sem, lw_sem, inside_sem, late_sem, up_sem,
):
    width = x_hbm.shape[1]
    rows = x_hbm.shape[0] // 2
    total = CHIPS * rows
    dom = lax.axis_index("dom")
    tm = lax.axis_index("tm")
    z, side = dom // 2, dom % 2
    across = dom + 1 - 2 * side
    other = 1 - tm

    def slot_of(d, q):
        high, low, turned = [
            here + there - 2 * here * there for here, there in ((z // 2, d // 2), (z % 2, d % 2), (side, q))
        ]
        return 4 * high + 2 * low + turned + tm * high * (turned - low)

    loads = [
        pltpu.make_async_copy(source, target, in_sem.at[i])
        for i, (source, target) in enumerate(
            [(lw_hbm, lw_held.at[0]), (w_hbm, w_ref), (p_hbm, p_ref), (x_hbm, held.at[0])]
        )
    ]
    barrier = pltpu.get_barrier_semaphore()

    def signal(sem, to_dom, to_tm):
        pl.semaphore_signal(sem, inc=1, device_id={"dom": to_dom, "tm": to_tm}, device_id_type=MESH)

    for d in range(1, 4):

        @pl.when(z < d)
        def _():
            for q in range(2):
                signal(barrier, 2 * d + q, tm)

    signal(barrier, across, tm)
    signal(barrier, dom, other)

    def remote(source, target, send, recv, to_dom, to_tm):
        return pltpu.make_async_remote_copy(
            src_ref=source,
            dst_ref=target,
            send_sem=send,
            recv_sem=recv,
            device_id={"dom": to_dom, "tm": to_tm},
            device_id_type=MESH,
        )

    def own(slot, to_dom):
        return (
            remote(lw_hbm, lw_held.at[slot], lw_send_sem.at[slot], lw_sem.at[slot], to_dom, tm),
            remote(x_hbm, held.at[slot], send_sem.at[slot], recv_sem.at[slot], to_dom, tm),
        )

    def start_own(d, q):
        def start():
            for copy in own(slot_of(d, q), 2 * d + q):
                copy.start()

        pl.when(sends_to(d, q))(start)

    def sends_to(d, q):
        crossed = side == q
        if d == 3:
            crossed = jnp.logical_and(crossed, z != 1)
        return jnp.logical_or(jnp.logical_or(z // 2 == d // 2, tm == 0), crossed)

    near = 2 * (z + 1 - 2 * (z % 2)) + side
    corner = 2 * (z + 1 - 2 * (z % 2)) + 1 - side

    def pass_on(source, slot, to_dom):
        index = CHIPS + 4 * (source - 4) + slot - 4
        return (
            remote(lw_held.at[source], lw_held.at[slot], lw_send_sem.at[index], lw_sem.at[slot], to_dom, tm),
            remote(held.at[source], held.at[slot], send_sem.at[index], recv_sem.at[slot], to_dom, tm),
        )

    def passes(do, ready):
        def run(source, *ways):
            ready(source)
            for slot, to_dom in ways:
                for copy in pass_on(source, slot, to_dom):
                    do(copy)

        @pl.when(z < 2)
        def _():
            run(4, (6, across))
            run(5, (7, across))

        @pl.when(z == 2)
        def _():
            run(5, (4, near), (6, corner), (7, across))
            run(4, (6, across))

        @pl.when(z == 3)
        def _():
            run(5, (7, across))
            ready(4)

    def middle(slot):
        source = x_hbm if slot == 0 else held.at[slot]
        return remote(
            source.at[0:rows], middle_rows.at[slot], inside_send_sem.at[slot], inside_sem.at[slot], dom, other
        )

    lean_copy = remote(lean, lean, inside_send_sem.at[CHIPS], late_sem.at[0], dom, other)
    score_copy = remote(score_mine, score_theirs, inside_send_sem.at[CHIPS + 1], late_sem.at[1], dom, other)

    pl.semaphore_wait(barrier, 2 + 2 * z)
    for d in range(3):

        @pl.when(z > d)
        def _():
            for q in range(2):
                signal(up_sem.at[slot_of(d, q)], 2 * d + q, tm)

    for d, turn_of in ((0, tm >= 0), (1, tm == 1), (2, tm >= 0), (1, tm == 0)):

        @pl.when(jnp.logical_and(z > d, turn_of))
        def _():
            for q in range(2):
                start_own(d, q)

    for copy in own(1, across):
        copy.start()

    @pl.when(tm == 1)
    def _():
        middle(0).start()

    for load in loads:
        load.start()

    for d in range(1, 4):

        @pl.when(z < d)
        def _():
            for q in range(2):
                pl.semaphore_wait(up_sem.at[slot_of(d, q)], 1)
                start_own(d, q)

    stage[...] = jnp.zeros_like(stage)
    for load in loads:
        load.wait()

    def arrive(slot):
        for copy in own(slot, across):
            copy.wait_recv()

    weight = w_ref[...]
    p_row = p_ref[...]
    p_down = jnp.broadcast_to(p_row, (width, width)).T
    scaled = jnp.concatenate(split_three(p_down * weight.astype(jnp.float32)), axis=1)
    line = lax.broadcasted_iota(jnp.int32, (EXTRA, 2 * width), 0)
    which = lax.broadcasted_iota(jnp.int32, (EXTRA, 2 * width), 1) // width
    pick = jnp.where((line < 6) & (line % 2 == which), 1.0, 0.0).astype(jnp.bfloat16)

    def flat(block):
        return block.reshape(block.shape[0] * rows, width)

    def columns_of(e, first, last):
        return flat(held[first:last, e * rows : (e + 1) * rows, :])

    def rows_of(e, first, last):
        return flat(middle_rows[first:last] if e else held[first:last, rows:, :])

    def spread_logs(first, last):
        for r in range(first, last):
            for n, value in enumerate(split_three(lw_held[r])):
                stage[2 * n : 2 * n + 2, r * width : r * width + rows] = value.astype(jnp.float32)
        spread = tn_dot(stage[:, first * width : last * width].astype(jnp.bfloat16), pick)
        for r in range(first, last):
            at = (r - first) * width
            for e in range(2):
                bias[e, r * rows : (r + 1) * rows, :] = spread[at : at + rows, e * width : (e + 1) * width]

    def prepare_columns(e, first, last):
        span = slice(first * rows, last * rows)
        mean = nt_dot(columns_of(e, first, last), weight)
        predicted[e, span, :] = mean
        energy = jnp.sum(p_row * mean * mean, axis=1, keepdims=True)
        bias[e, span, :] = bias[e, span, :] - 0.5 * energy

    def prepare_rows(e, first, last):
        wide = nn_dot(rows_of(e, first, last), scaled)
        projected[e, first * rows : last * rows, :] = (
            wide[:, :width] + (wide[:, width : 2 * width] + wide[:, 2 * width :])
        ).astype(jnp.bfloat16)

    class Cut:
        def __init__(self, e, columns, lanes):
            self.e, self.first = e, lanes * rows // width * width
            self.ranks = ((0, columns), (columns, CHIPS))
            self.spans = [slice(a * rows, b * rows) for a, b in self.ranks]

    def exponentials(e, first, last, lanes):
        span = slice(first * rows, last * rows)
        scores = nt_dot(columns_of(e, first, last), projected[e, lanes, :])
        scores = scores + jnp.concatenate([bias[e, span, :]] * ((lanes.stop - lanes.start) // width), axis=1)
        top = jnp.max(scores, axis=0, keepdims=True)
        terms = jnp.exp(scores - top)
        kernel_rows[e, span, lanes] = terms.astype(jnp.bfloat16)
        return top, jnp.sum(terms, axis=0, keepdims=True)

    def tile(cut, c):
        e, lanes = cut.e, slice(0, cut.first)
        top, norm = exponentials(e, *cut.ranks[c], lanes)
        stats[e, c, 0:1, lanes] = top
        stats[e, c, 1:2, lanes] = norm

    def tall_tile(cut):
        e, lanes = cut.e, slice(cut.first, total)
        top, norm = exponentials(e, 0, CHIPS, lanes)
        stats[e, 0, 0:1, lanes] = top
        stats[e, 0, 1:2, lanes] = norm

    def turn(row):
        return jnp.broadcast_to(row, (width, width)).T

    def blocks(lanes):
        return [slice(at, at + width) for at in range(lanes.start, lanes.stop, width)]

    def normalize(cut):
        e, lanes = cut.e, slice(0, cut.first)
        tops = [stats[e, c, 0:1, lanes] for c in range(2)]
        top = jnp.maximum(tops[0], tops[1])
        scales = [jnp.exp(tops[c] - top) for c in range(2)]
        norm = sum(scales[c] * stats[e, c, 1:2, lanes] for c in range(2))
        for c in range(2):
            inverse = scales[c] / norm
            for block in blocks(lanes):
                inverse_norm[e, c, block, :] = turn(inverse[:, block])
        lanes = slice(cut.first, total)
        inverse = 1.0 / stats[e, 0, 1:2, lanes]
        for block, source in zip(blocks(lanes), blocks(slice(0, total - cut.first))):
            inverse_norm[e, 0, block, :] = turn(inverse[:, source])

    def ratios(cut, came):
        e, lanes, rest = cut.e, slice(0, cut.first), slice(cut.first, total)
        below = weights[came, rest, :] * inverse_norm[e, 0, rest, :]
        return [
            jnp.concatenate([weights[came, lanes, :] * inverse_norm[e, c, lanes, :], below], axis=0)
            for c in range(2)
        ]

    def weigh(cut, came, gives):
        e, spans, ranks = cut.e, cut.spans, cut.ranks
        for c, ratio in enumerate(ratios(cut, came)):
            weights[gives, spans[c], :] = nn_dot(kernel_rows[e, spans[c], :], ratio.astype(jnp.bfloat16))

    def move(cut, came):
        e, spans, ranks = cut.e, cut.spans, cut.ranks
        later = rows_of(e, 0, CHIPS).astype(jnp.float32)
        return [
            nn_dot(kernel_rows[e, spans[c], :], (ratio * later).astype(jnp.bfloat16))
            for c, ratio in enumerate(ratios(cut, came))
        ]

    def step_back(cut, came, gives):
        e, spans, ranks = cut.e, cut.spans, cut.ranks
        later = rows_of(e, 0, CHIPS).astype(jnp.float32)
        moved = []
        for c, ratio in enumerate(ratios(cut, came)):
            right = jnp.concatenate(
                [(ratio * later).astype(jnp.bfloat16), ratio.astype(jnp.bfloat16)], axis=1
            )
            both = nn_dot(kernel_rows[e, spans[c], :], right)
            weights[gives, spans[c], :] = both[:, width:]
            moved.append(both[:, :width])
        return moved

    def gradient(cut, moved, gives):
        e, spans, ranks = cut.e, cut.spans, cut.ranks
        part = jnp.zeros((width, width), jnp.float32)
        for c in range(2):
            residual = moved[c] - predicted[e, spans[c], :] * weights[gives, spans[c], :]
            part = part + tn_dot(residual.astype(jnp.bfloat16), columns_of(e, *ranks[c]))
        return part

    def hand_on():
        passes(lambda copy: copy.start(), arrive)
        for slot in range(4, EARLY):
            middle(slot).start()

    pl.when(jnp.logical_and(tm == 1, z == 2))(hand_on)
    for slot in range(1, 4):
        arrive(slot)

        @pl.when(tm == 1)
        def _():
            middle(slot).start()

    @pl.when(tm == 1)
    def _():
        cut = Cut(0, EARLY, EARLY)
        pl.when(z != 2)(hand_on)
        spread_logs(0, EARLY)
        prepare_columns(0, 0, EARLY)
        prepare_rows(0, 0, EARLY)
        tile(cut, 0)
        for slot in range(EARLY, CHIPS):
            arrive(slot)
            middle(slot).start()
        spread_logs(EARLY, CHIPS)
        prepare_columns(0, EARLY, CHIPS)
        prepare_rows(0, EARLY, CHIPS)
        tile(cut, 1)
        tall_tile(cut)
        normalize(cut)
        last = jnp.exp(bias[1] - jnp.max(bias[1], axis=0, keepdims=True))
        weights[1] = last / jnp.sum(last, axis=0, keepdims=True)
        weigh(cut, 1, 0)
        for b, block in enumerate(blocks(slice(0, total))):
            lean[b : b + 1, :] = weights[0, block, :].T[0:1, :]
        lean_copy.start()
        score_mine[...] = gradient(cut, move(cut, 1), 0)

    @pl.when(tm == 0)
    def _():
        zero, one = Cut(0, 4, 4), Cut(1, 4, LANES_ONE)
        spread_logs(0, 4)
        for e in range(2):
            prepare_columns(e, 0, 4)
        prepare_rows(0, 0, 4)
        tile(zero, 0)
        for slot in range(LANES_ONE):
            middle(slot).wait_recv()
        prepare_rows(1, 0, LANES_ONE)
        tile(one, 0)
        for slot in range(4, CHIPS):
            arrive(slot)
        spread_logs(4, CHIPS)
        for e in range(2):
            prepare_columns(e, 4, CHIPS)
        prepare_rows(0, 4, CHIPS)
        tile(one, 1)
        tile(zero, 1)
        for slot in range(LANES_ONE, CHIPS):
            middle(slot).wait_recv()
        prepare_rows(1, LANES_ONE, CHIPS)
        tall_tile(one)
        tall_tile(zero)
        normalize(one)
        normalize(zero)
        lean_copy.wait_recv()
        for b, block in enumerate(blocks(slice(0, total))):
            weights[2, block, :] = turn(lean[b : b + 1, :])
        first_moved = step_back(one, 2, 1)
        moved = step_back(zero, 1, 0)
        score_mine[...] = gradient(one, first_moved, 1) + gradient(zero, moved, 0)

    score_copy.start()
    for k in range(2):
        smoothed_ref[k : k + 1, :] = weights[k, 0:rows, :].T[0:1, :] * total
    score_copy.wait_recv()
    score_ref[...] = (score_mine[...] + score_theirs[...]) * p_down

    for d in range(4):

        @pl.when(z != d)
        def _():
            for q in range(2):

                @pl.when(sends_to(d, q))
                def _():
                    for copy in own(slot_of(d, q), 2 * d + q):
                        copy.wait_send()

    for copy in own(1, across):
        copy.wait_send()
    score_copy.wait_send()

    @pl.when(tm == 1)
    def _():
        passes(lambda copy: copy.wait_send(), lambda slot: None)
        for slot in range(CHIPS):
            middle(slot).wait_send()
        lean_copy.wait_send()


def hand_over(a_in, b_in, a_out, b_out, sems):
    leaving = [
        pltpu.make_async_copy(a_in, a_out, sems.at[0]),
        pltpu.make_async_copy(b_in, b_out, sems.at[1]),
    ]
    for copy in leaving:
        copy.start()
    for copy in leaving:
        copy.wait()


def fused(particles, log_weight, trans_weight, precision):
    steps_here, rows, width = particles.shape
    total = CHIPS * rows
    whole = pl.BlockSpec(memory_space=pltpu.VMEM)
    arguments = (
        particles.reshape(steps_here * rows, width), log_weight, trans_weight, precision.reshape(1, width)
    )
    smoothed, score = pl.pallas_call(
        smoother_kernel,
        out_shape=(
            pltpu.VMEM((steps_here, rows), jnp.float32),
            pltpu.VMEM((width, width), jnp.float32),
        ),
        in_specs=[pl.BlockSpec(memory_space=pltpu.HBM)] * 4,
        out_specs=(whole, whole),
        scratch_shapes=[
            pltpu.VMEM((CHIPS, steps_here, rows), jnp.float32),
            pltpu.VMEM((width, width), jnp.bfloat16),
            pltpu.VMEM((1, width), jnp.float32),
            pltpu.VMEM((CHIPS, 2 * rows, width), jnp.bfloat16),
            pltpu.VMEM((CHIPS, rows, width), jnp.bfloat16),
            pltpu.VMEM((2, total, total), jnp.bfloat16),
            pltpu.VMEM((2, 2, 8, total), jnp.float32),
            pltpu.VMEM((2, 2, total, width), jnp.float32),
            pltpu.VMEM((2, total, width), jnp.float32),
            pltpu.VMEM((2, total, width), jnp.bfloat16),
            pltpu.VMEM((2, total, width), jnp.float32),
            pltpu.VMEM((3, total, width), jnp.float32),
            pltpu.VMEM((EXTRA, CHIPS * width), jnp.float32),
            pltpu.VMEM((8, width), jnp.float32),
            pltpu.VMEM((width, width), jnp.float32),
            pltpu.VMEM((width, width), jnp.float32),
            pltpu.SemaphoreType.DMA((4,)),
            pltpu.SemaphoreType.DMA((2 * CHIPS,)),
            pltpu.SemaphoreType.DMA((2 * CHIPS,)),
            pltpu.SemaphoreType.DMA((CHIPS + 2,)),
            pltpu.SemaphoreType.DMA((CHIPS,)),
            pltpu.SemaphoreType.DMA((CHIPS,)),
            pltpu.SemaphoreType.DMA((CHIPS,)),
            pltpu.SemaphoreType.DMA((2,)),
            pltpu.SemaphoreType.REGULAR((CHIPS,)),
        ],
        compiler_params=pltpu.CompilerParams(
            collective_id=0, has_side_effects=True, vmem_limit_bytes=40 * 2**20
        ),
    )(*[pltpu.with_memory_space_constraint(a, pltpu.HBM) for a in arguments])
    return pl.pallas_call(
        hand_over,
        out_shape=(
            jax.ShapeDtypeStruct((steps_here, rows), jnp.float32),
            jax.ShapeDtypeStruct((width, width), jnp.float32),
        ),
        in_specs=[whole] * 2,
        out_specs=(pl.BlockSpec(memory_space=pltpu.HBM),) * 2,
        scratch_shapes=[
            pltpu.SemaphoreType.DMA((2,)),
        ],
        compiler_params=pltpu.CompilerParams(vmem_limit_bytes=40 * 2**20),
    )(smoothed, score)


def plan(particles, log_weight, trans_weight, precision):
    steps_here, rows, width = particles.shape
    n_dom = lax.axis_size("dom")
    total = n_dom * rows
    small = total <= MOST_ROWS and total % (2 * width) == 0 and rows <= width and rows % 16 == 0
    shaped = n_dom == 8 and lax.axis_size("tm") == 2 and steps_here == 2 and width == 128
    if small and shaped:
        return fused(particles, log_weight, trans_weight, precision)
    return shards(particles, log_weight, trans_weight, precision)


def solution(mesh):
    placed = (P("tm", ("seq", "dom"), None), P("tm", ("seq", "dom")), P(), P())
    return jax.shard_map(
        plan,
        mesh=mesh,
        in_specs=placed,
        out_specs=(P("tm", ("seq", "dom")), P("seq", None)),
        check_vma=False,
    )
```
